128 devices in a mesh: row: 4 (over y_lo, core), col: 32 (over y_hi, x, z).
Axes of the slice: x: 4, y: 4 (y_hi: 2, y_lo: 2; y = y_hi * 2 + y_lo), z: 4, core: 2. Of those that a mesh axis runs over, the one named last changes fastest.
Arguments:
- row_coords: bfloat16 [3, 4096, 512], P(None, ('row', 'col')), may hold values from -10 to 10, as said below
- col_coords: bfloat16 [3, 32768, 512], P(None, 'col'), may hold values from -10 to 10, as said below
- start_block: float32 [32768, 64], P('col'), may hold values from -0.03125 to 0.03125
Outputs:
- basis: float32 [4096, 64], P('row')
- image: float32 [32768, 64], P('col')
The draws below stay inside these ranges and needn't reach their ends.
Inputs may be any that keep to these rules, and one draw needn't show every extreme that they name: `row_coords`: coordinates of frames of one molecule in varying conformations. `col_coords`: coordinates of frames of the same molecule in varying conformations.
All inputs are finite; a program needn't handle non-finite values.
Results may differ from the reference program's by a relative error of at most 0.0073.
Values may be sent and summed in bfloat16 or wider, within the bound.
No kernel may reach another device: no remote copies, remote signals or barrier semaphores. Data moves between devices by JAX's collectives and lax.ppermute only.
A program may use at most 128 MiB of HBM per device.

```python
import math
import jax
import jax.numpy as jnp
from jax import lax

ATOMS = 512
K = 64
NEWTON = 8
C_DEV = 1024
RF = 4096
CF = 32768
N_COL = 32


def shared_structure(key):
    base = jnp.clip(jax.random.normal(jax.random.fold_in(key, 7), (3, ATOMS), jnp.float32), -4.0, 4.0)
    base = base - jnp.mean(base, axis=1, keepdims=True)
    mode = jnp.clip(jax.random.normal(jax.random.fold_in(key, 9), (3, ATOMS), jnp.float32), -4.0, 4.0)
    mode = mode - jnp.mean(mode, axis=1, keepdims=True)
    base = base * jnp.array([2.0, 0.35, 0.25], jnp.float32)[:, None]
    mode = mode * 0.5
    return (base, mode)


def moving_frames(key, count, salt):
    base, mode = shared_structure(key)
    inner = jax.random.fold_in(key, salt)
    quats = jax.random.normal(jax.random.fold_in(inner, 1), (count, 4), jnp.float32)
    quats = quats / (jnp.sqrt(jnp.sum(quats * quats, axis=1, keepdims=True)) + 1e-06)
    qw, qx, qy, qz = (quats[:, 0], quats[:, 1], quats[:, 2], quats[:, 3])
    rotation = jnp.stack([jnp.stack([1 - 2 * (qy * qy + qz * qz), 2 * (qx * qy - qz * qw), 2 * (qx * qz + qy * qw)], axis=1), jnp.stack([2 * (qx * qy + qz * qw), 1 - 2 * (qx * qx + qz * qz), 2 * (qy * qz - qx * qw)], axis=1), jnp.stack([2 * (qx * qz - qy * qw), 2 * (qy * qz + qx * qw), 1 - 2 * (qx * qx + qy * qy)], axis=1)], axis=1)
    noise = jnp.clip(jax.random.normal(jax.random.fold_in(inner, 2), (3, count, ATOMS), jnp.float32), -4.0, 4.0)
    amplitude = jax.random.uniform(jax.random.fold_in(inner, 4), (count,), jnp.float32, -1.0, 1.0)
    shape = base[None, :, :] + amplitude[:, None, None] * mode[None, :, :]
    position = jnp.arange(count, dtype=jnp.float32) / count
    spread = jax.random.uniform(jax.random.fold_in(inner, 3), (count,), jnp.float32, 1.0, 1.6)
    jitter = jnp.exp(jax.random.uniform(jax.random.fold_in(inner, 5), (count,), jnp.float32, 0.0, 0.9162907))
    sigma = 0.2 * jnp.exp(position * 1.0986123) * spread * jitter
    rotated = jnp.einsum('fcd,fda->cfa', rotation, shape)
    moved = rotated + sigma[None, :, None] * noise
    return jnp.clip(moved, -10.0, 10.0).astype(jnp.bfloat16)


def draw_row_coords(key, part):
    return moving_frames(key, RF, 11)


def draw_col_coords(key, part):
    return moving_frames(key, CF, 13)


def block_scale(key, extent, cuts, least, largest):
    level, own = 1.0, jax.random.fold_in(key, 6)
    for dim, parts in cuts:
        steps = jnp.exp(jax.random.uniform(jax.random.fold_in(own, dim), (parts,), jnp.float32, least / len(cuts), largest / len(cuts)))
        level = level * jnp.repeat(steps, extent[dim] // parts).reshape([-1 if axis == dim else 1 for axis in range(len(extent))])
    return level


def bell_draw(rng, shape, width, limit, pieces=(), kind=jnp.bfloat16):
    loudness = block_scale(rng, shape, pieces, -0.22, 0.18) if pieces else 1.0
    values = jax.random.normal(rng, shape, jnp.float32) * width * loudness
    return jnp.minimum(jnp.maximum(values, -limit), limit).astype(kind)


def setup_inputs(seed: int = 0) -> dict:
    arg_keys = jax.random.split(jax.random.key(seed), 4)
    row_coords = draw_row_coords(jax.random.fold_in(arg_keys[3], 71), 0)
    col_coords = draw_col_coords(jax.random.fold_in(arg_keys[3], 71), 0)
    start_block = bell_draw(arg_keys[2], (CF, K), CF ** -0.5, 0.03125, ((0, 32),), jnp.float32)
    return dict(row_coords=row_coords, col_coords=col_coords, start_block=start_block)


def centre_frames(coords):
    shifted = coords.astype(jnp.float32)
    shifted = shifted - lax.optimization_barrier(jnp.mean(shifted, axis=2, keepdims=True))
    rounded = shifted.astype(jnp.bfloat16)
    widened = lax.optimization_barrier(rounded).astype(jnp.float32)
    return (rounded, lax.optimization_barrier(jnp.sum(widened * widened, axis=(0, 2))) / ATOMS)

def two_minor(matrix, upper, lower, left, right):
    return matrix[upper][left] * matrix[lower][right] - matrix[lower][left] * matrix[upper][right]

def squared_rmsd(cross, row_norm, col_norm):
    part = [[cross[first, second] for second in range(3)] for first in range(3)]
    trace = part[0][0] + part[1][1] + part[2][2]
    matrix = [[None] * 4 for index in range(4)]
    matrix[0][0] = trace
    matrix[1][1] = 2.0 * part[0][0] - trace
    matrix[2][2] = 2.0 * part[1][1] - trace
    matrix[3][3] = 2.0 * part[2][2] - trace
    matrix[0][1] = part[1][2] - part[2][1]
    matrix[0][2] = part[2][0] - part[0][2]
    matrix[0][3] = part[0][1] - part[1][0]
    matrix[1][2] = part[0][1] + part[1][0]
    matrix[1][3] = part[2][0] + part[0][2]
    matrix[2][3] = part[1][2] + part[2][1]
    for first in range(4):
        for second in range(first):
            matrix[first][second] = matrix[second][first]
    key_determinant = two_minor(matrix, 0, 1, 0, 1) * two_minor(matrix, 2, 3, 2, 3) - two_minor(matrix, 0, 1, 0, 2) * two_minor(matrix, 2, 3, 1, 3) + two_minor(matrix, 0, 1, 0, 3) * two_minor(matrix, 2, 3, 1, 2) + two_minor(matrix, 0, 1, 1, 2) * two_minor(matrix, 2, 3, 0, 3) - two_minor(matrix, 0, 1, 1, 3) * two_minor(matrix, 2, 3, 0, 2) + two_minor(matrix, 0, 1, 2, 3) * two_minor(matrix, 2, 3, 0, 1)
    cross_determinant = part[0][0] * (part[1][1] * part[2][2] - part[1][2] * part[2][1]) - part[0][1] * (part[1][0] * part[2][2] - part[1][2] * part[2][0]) + part[0][2] * (part[1][0] * part[2][1] - part[1][1] * part[2][0])
    squares = sum((part[first][second] * part[first][second] for first in range(3) for second in range(3)))
    coeff_two = -2.0 * squares
    coeff_one = -8.0 * cross_determinant
    coeff_zero = key_determinant
    root_guess = 0.5 * (row_norm + col_norm)
    for sweep in range(NEWTON):
        poly_value = ((root_guess * root_guess + coeff_two) * root_guess + coeff_one) * root_guess + coeff_zero
        poly_slope = (4.0 * root_guess * root_guess + 2.0 * coeff_two) * root_guess + coeff_one
        root_guess = root_guess - poly_value / poly_slope
    return row_norm + col_norm - 2.0 * root_guess

def reference(row_coords, col_coords, start_block):
    highest = lax.Precision.HIGHEST
    rows, row_norm = centre_frames(row_coords)
    cols, col_norm = centre_frames(col_coords)
    rows_wide = rows.astype(jnp.float32)
    col_blocks = cols.reshape(3, N_COL, C_DEV, ATOMS).transpose(1, 0, 2, 3)
    norm_blocks = col_norm.reshape(N_COL, C_DEV)

    def tile(inputs):
        block, norms = inputs
        cross = jnp.einsum('ark,bck->abrc', rows_wide, block.astype(jnp.float32)) / ATOMS
        return squared_rmsd(cross, row_norm[:, None], norms[None, :])
    stacked = lax.map(tile, (col_blocks, norm_blocks))
    dist = stacked.transpose(1, 0, 2).reshape(RF, CF)
    row_mean = lax.optimization_barrier(jnp.sum(dist, axis=1)) / CF
    col_mean = lax.optimization_barrier(jnp.sum(dist, axis=0)) / RF
    grand = jnp.sum(row_mean) / RF
    centred = -0.5 * (dist - row_mean[:, None] - col_mean[None, :] + grand)
    panel = jnp.dot(centred, start_block, precision=highest)
    gram = jnp.dot(panel.T, panel, precision=highest) / RF
    lower = jnp.linalg.cholesky(gram)
    basis = lax.linalg.triangular_solve(lower, panel, left_side=False, lower=True, transpose_a=True)
    image = jnp.dot(centred.T, basis, precision=highest) / math.sqrt(RF)
    return (basis, image)
```

```python
import functools

import jax
import jax.numpy as jnp
from jax import lax
from jax.experimental import pallas as pl
from jax.experimental.pallas import tpu as pltpu
from jax.sharding import PartitionSpec as P

ATOMS = 512
NEWTON = 8
K = 64
TR = 128
TC = 256
RF = 4096
CF = 32768
HIGHEST = lax.Precision.HIGHEST
OFFSETS = (0, -1, 1, 2)


def centred(coords):
    wide = coords.astype(jnp.float32)
    wide = wide - jnp.mean(wide, axis=2, keepdims=True)
    return lax.reduce_precision(wide, 8, 7)


def newton_slice(p, u):
    def g(i, j):
        return p[0][i] * p[0][j] + p[1][i] * p[1][j] + p[2][i] * p[2][j]

    g00, g11, g22, g01, g02, g12 = g(0, 0), g(1, 1), g(2, 2), g(0, 1), g(0, 2), g(1, 2)
    det = (
        p[0][0] * (p[1][1] * p[2][2] - p[1][2] * p[2][1])
        - p[0][1] * (p[1][0] * p[2][2] - p[1][2] * p[2][0])
        + p[0][2] * (p[1][0] * p[2][1] - p[1][1] * p[2][0])
    )
    q = g00 + g11 + g22
    cross = g01 * g01 + g02 * g02 + g12 * g12
    square = g00 * g00 + g11 * g11 + g22 * g22 + (cross + cross)
    half = 0.5 * q
    rest = half * half - 0.5 * square
    twice = det + det
    x = u
    for _ in range(NEWTON):
        s = x * x
        x = ((0.75 * s - half) * s + rest) / ((s - q) * x - twice)
    return u - x


def dist_kernel(nb, *refs):
    rows = refs[:nb]
    cols, cn, sw = refs[nb : nb + 3]
    hi, lo, t_out = refs[nb + 3 : nb + 6]
    bufs, rn = refs[nb + 6 : nb + 8], refs[nb + 8]
    ct = pl.program_id(0)
    last = pl.num_programs(0) - 1

    def products(rb, at, buf):
        c0 = pl.multiple_of(at * TC, TC)
        lhs = rows[rb][...].reshape(3 * TR, ATOMS)
        for b in range(3):
            buf[b] = lax.dot_general(
                lhs, cols[b, pl.ds(c0, TC), :], (((1,), (1,)), ((), ())), preferred_element_type=jnp.float32
            )

    @pl.when(ct == 0)
    def _():
        t_out[...] = jnp.zeros_like(t_out)
        for rb in range(nb):
            w = rows[rb][...].astype(jnp.float32)
            n = jnp.sum(jnp.sum(w * w, axis=0), axis=1, keepdims=True) * (2.0 / ATOMS)
            rn[rb] = jnp.broadcast_to(n, (TR, 128))
        products(0, 0, bufs[0])

    for rb in range(nb):
        after, at = (rb + 1, ct) if rb + 1 < nb else (0, jnp.minimum(ct + 1, last))
        products(after, at, bufs[(rb + 1) % 2])
        buf = bufs[rb % 2]
        for r in range(0, TR, 16):
            for c in range(0, TC, 128):
                p = [[buf[b, a * TR + r : a * TR + r + 16, c : c + 128] for b in range(3)] for a in range(3)]
                u = rn[rb, r : r + 16] + cn[0, 0:1, c : c + 128]
                d = newton_slice(p, u)
                h = d.astype(jnp.bfloat16)
                hi[rb * TR + r : rb * TR + r + 16, c : c + 128] = h
                lo[rb * TR + r : rb * TR + r + 16, c : c + 128] = (d - h.astype(jnp.float32)).astype(jnp.bfloat16)
    w = sw[pl.ds(pl.multiple_of(ct * TC, TC), TC), :]
    t_out[...] += jnp.dot(hi[...], w, preferred_element_type=jnp.float32)
    t_out[...] += jnp.dot(lo[...], w, preferred_element_type=jnp.float32)


def whole(a):
    return pl.BlockSpec(a.shape, lambda *_: (0,) * a.ndim)


def dist_call(blocks, cols, cn, sw):
    nb, nc = len(blocks), cols.shape[1]
    r = nb * TR
    return pl.pallas_call(
        functools.partial(dist_kernel, nb),
        grid=(nc // TC,),
        in_specs=[whole(b) for b in blocks] + [whole(cols), pl.BlockSpec((1, 1, TC), lambda c: (c, 0, 0)), whole(sw)],
        out_specs=[
            pl.BlockSpec((r, TC), lambda c: (0, c)),
            pl.BlockSpec((r, TC), lambda c: (0, c)),
            pl.BlockSpec((r, 256), lambda c: (0, 0)),
        ],
        out_shape=[
            jax.ShapeDtypeStruct((r, nc), jnp.bfloat16),
            jax.ShapeDtypeStruct((r, nc), jnp.bfloat16),
            jax.ShapeDtypeStruct((r, 256), jnp.float32),
        ],
        scratch_shapes=[
            pltpu.VMEM((3, 3 * TR, TC), jnp.float32),
            pltpu.VMEM((3, 3 * TR, TC), jnp.float32),
            pltpu.VMEM((nb, TR, 128), jnp.float32),
        ],
        compiler_params=pltpu.CompilerParams(dimension_semantics=("arbitrary",), vmem_limit_bytes=24 << 20),
        cost_estimate=pl.CostEstimate(
            flops=r * nc * 9 * 2 * ATOMS, bytes_accessed=8 << 20, transcendentals=r * nc * NEWTON
        ),
        name=f"dist{nb}",
    )(*blocks, cols, cn, sw)


BLOCK_OF = {
    0: ((0, 0), (1, 0), (1, 1), (2, 0)),
    1: ((0, 1), (1, 2), (1, 3), (2, 1)),
}


def place(half, dy, ix, iz):
    outer, inner = (ix, iz) if half == 0 else (iz, ix)
    chunk, block = BLOCK_OF[half][outer]
    return chunk, block * TR + (inner * 2 + dy) * 16


def owner_of(dy, ix, iz):
    me = lax.axis_index("col")
    y, x, z = me // 16, (me // 4) % 4, me % 4
    return ((y + dy) % 2) * 16 + ((x + OFFSETS[ix] + 4) % 4) * 4 + (z + OFFSETS[iz] + 4) % 4


PIECES = [(dy, ix, iz) for dy in range(2) for ix in range(4) for iz in range(4)]


def lanes(shape):
    return lax.broadcasted_iota(jnp.int32, shape, len(shape) - 1)


def pack_kernel(t0, t1, t2, bm, out):
    ts = (t0, t1, t2)
    lane16, lane8 = lanes((16, 128)), lanes((8, 128))
    means = jnp.broadcast_to(bm[...], (8, 128))
    for piece in PIECES:
        dest = owner_of(*piece)
        full, sums = [], []
        for half in range(2):
            chunk, r = place(half, *piece)
            t = ts[chunk][r : r + 16, 0:128]
            full.append(t + pltpu.roll(t, 64, 1))
            sums.append(ts[chunk][r : r + 16, 128:256])
        out[dest, 0:16, :] = jnp.where(lane16 < 64, full[0], full[1])
        ext = jnp.where(lane8 < 16, sums[0][0:8], sums[0][8:16])
        ext = jnp.where(lane8 < 32, ext, sums[1][0:8])
        ext = jnp.where(lane8 < 48, ext, sums[1][8:16])
        out[dest, 16:24, :] = jnp.where(lane8 < 64, ext, means)


def owner_kernel(got, out):
    lane = lanes((8, 128))

    def spread(ext):
        one = lambda k: jnp.broadcast_to(ext[:, k : k + 1], (8, 128))
        return jnp.where(lane < 64, one(0), one(32)), jnp.where(lane < 64, one(16), one(48))

    zero = jnp.zeros((8, 128), jnp.float32)
    a, b, e = zero, zero, zero
    for src in range(got.shape[0]):
        ext = got[src, 16:24, :]
        bm = jnp.where(lane < 64, pltpu.roll(ext, 64, 1), ext)
        r0, r1 = spread(ext)
        a = a + (got[src, 0:8, :] + r0 * bm)
        b = b + (got[src, 8:16, :] + r1 * bm)
        e = e + ext
    bm = jnp.where(lane < 64, pltpu.roll(e, 64, 1), e) * (1.0 / got.shape[0])
    r0, r1 = spread(e)
    a = a - r0 * bm
    b = b - r1 * bm
    sub = lax.broadcasted_iota(jnp.int32, (8, 128), 0)
    y = jnp.sum(r0 * a + r1 * b, axis=0, keepdims=True)
    tot = jnp.sum(r0 + r1, axis=0, keepdims=True)
    ext = jnp.where(sub == 0, jnp.broadcast_to(y, (8, 128)), jnp.broadcast_to(tot, (8, 128)))
    for dst in range(got.shape[0]):
        out[dst, 0:8, :] = a
        out[dst, 8:16, :] = b
        out[dst, 16:24, :] = ext


def panel_kernel(got, left, tc_out, stat, arr):
    n = got.shape[0]
    lane1 = lanes((1, 128))

    def both(v):
        return v + pltpu.roll(v, 64, 1)

    total = jnp.sum(jnp.sum(got[:, 0:16, :], axis=0), axis=0, keepdims=True)
    mean = both(total) * (1.0 / (32 * n))
    ext = jnp.sum(got[:, 16:24, :], axis=0)
    y, rows = both(ext[0:1]), both(ext[1:2])
    x = got[:, 0:16, :] - mean
    flat = x.reshape(n * 16, 128)
    g = lax.dot_general(flat, flat, (((0,), (0,)), ((), ())), precision=HIGHEST, preferred_element_type=jnp.float32)
    stat[0:64, :] = g[0:64, :] + pltpu.roll(g[64:128, :], 64, 1)
    sub = lax.broadcasted_iota(jnp.int32, (8, 128), 0)
    tile = jnp.where(sub == 0, mean, jnp.where(sub == 1, y, rows))
    stat[64:72, :] = jnp.broadcast_to(tile, (8, 128))
    for b in range(n):
        tc_out[b * 32 : b * 32 + 16, :] = x[b, :, 0:64]
        tc_out[b * 32 + 16 : b * 32 + 32, :] = x[b, :, 64:128]
    start = (0, 256, 768)
    for piece in PIECES:
        src = owner_of(*piece)
        t = got[src, 0:16, :] - mean
        for half in range(2):
            chunk, r = place(half, *piece)
            arr[start[chunk] + r : start[chunk] + r + 16, :] = t if half == 0 else pltpu.roll(t, 64, 1)
    pt = jnp.transpose(arr[...])[0:64, :]
    h = pt.astype(jnp.bfloat16)
    left[0:64, :] = h
    left[64:128, :] = (pt - h.astype(jnp.float32)).astype(jnp.bfloat16)
    left[128:144, :] = jnp.ones((16, pt.shape[1]), jnp.bfloat16)


def image_kernel(me, left, h0, l0, h1, l1, h2, l2, out):
    acc = jnp.zeros((144, TC), jnp.float32)
    for at, refs in ((0, (h0, l0)), (256, (h1, l1)), (768, (h2, l2))):
        for ref in refs:
            acc += jnp.dot(left[:, at : at + ref.shape[0]], ref[...], preferred_element_type=jnp.float32)
    out[0, 0:64, :] = acc[0:64] + acc[64:128]
    out[0, 64:72, :] = acc[128:136]


def image_call(me, left, chunks):
    flat = [a for c in chunks for a in c[:2]]
    spec = lambda a: pl.BlockSpec((a.shape[0], TC), lambda k, me: (0, me[0] ^ k))
    return pl.pallas_call(
        image_kernel,
        grid_spec=pltpu.PrefetchScalarGridSpec(
            num_scalar_prefetch=1,
            grid=(4,),
            in_specs=[pl.BlockSpec(left.shape, lambda k, me: (0, 0))] + [spec(a) for a in flat],
            out_specs=pl.BlockSpec((1, 72, TC), lambda k, me: (k, 0, 0)),
        ),
        out_shape=jax.ShapeDtypeStruct((4, 72, TC), jnp.float32),
        compiler_params=pltpu.CompilerParams(dimension_semantics=("arbitrary",), vmem_limit_bytes=24 << 20),
        cost_estimate=pl.CostEstimate(flops=2 * 2 * 256 * 1024 * 1024, bytes_accessed=5 << 20, transcendentals=0),
        name="image",
    )(me, left, *flat)


def factor_kernel(s0, s1, s2, s3, m_out, d_out):
    stats = (s0, s1, s2, s3)

    def total(lo, hi):
        return (s0[lo:hi, :] + s1[lo:hi, :]) + (s2[lo:hi, :] + s3[lo:hi, :])

    mean = total(64, 65) * 0.25
    offs = [s[64:65, :] - mean for s in stats]
    y = total(65, 66) - mean * total(66, 67)
    sub = lax.broadcasted_iota(jnp.int32, (8, 128), 0)
    deltas = jnp.zeros((8, 128), jnp.float32)
    for k in range(4):
        deltas = jnp.where(sub == k, offs[k], deltas)
    d_out[...] = jnp.where(sub == 4, y * (1.0 / CF), deltas)
    outer = lax.dot_general(
        deltas, deltas, (((0,), (0,)), ((), ())), precision=HIGHEST, preferred_element_type=jnp.float32
    )
    gram = (total(0, 64) + outer[0:64, :] * (RF // 4)) * (1.0 / (16 * RF))
    lane = lanes((64, 128))
    row = lax.broadcasted_iota(jnp.int32, (64, 128), 0)
    a = jnp.where(lane < 64, gram, jnp.where(lane - 64 == row, 1.0, 0.0))
    scale = jnp.zeros((64, 1), jnp.float32)
    row1 = lax.broadcasted_iota(jnp.int32, (64, 1), 0)
    for k in range(64):
        pivot = a[k : k + 1, k : k + 1]
        scale = jnp.where(row1 == k, lax.rsqrt(pivot), scale)
        times = jnp.where(row1 > k, a[:, k : k + 1] / pivot, 0.0)
        a = a - times * a[k : k + 1, :]
    m_out[...] = a * (scale * -0.25)


def join_kernel(w, g1, g2, g3, m, d, out):
    parts = ((w[0, 0:64] + g1[0, 0:64]) + (g2[0, 0:64] + g3[0, 0:64]))
    sub = lax.broadcasted_iota(jnp.int32, (8, TC), 0)
    sums = jnp.where(sub == 4, -1.0, 0.0)
    for k, ref in enumerate((w, g1, g2, g3)):
        sums = jnp.where(sub == k, ref[0, 64:72], sums)
    add = lax.dot_general(
        d[...], sums, (((0,), (0,)), ((), ())), precision=HIGHEST, preferred_element_type=jnp.float32
    )
    inv = pltpu.roll(m[...], 64, 1)[:, 0:64]
    res = jnp.dot(inv, parts + add[0:64], precision=HIGHEST, preferred_element_type=jnp.float32)
    out[...] = (res * (-0.25 / RF**0.5)).astype(jnp.bfloat16)


def basis_kernel(tc, m, d, out):
    inv = pltpu.roll(m[...], 64, 1)[:, 0:64]
    x = tc[...] + d[0:1, 0:64]
    out[...] = lax.dot_general(
        x, inv, (((1,), (1,)), ((), ())), precision=HIGHEST, preferred_element_type=jnp.float32
    )


def spread_kernel(i0, i1, i2, i3, out):
    me = lax.axis_index("row")
    for k, ref in enumerate((i0, i1, i2, i3)):
        at = pl.multiple_of((me ^ k) * TC, TC)
        out[pl.ds(at, TC), :] = jnp.transpose(ref[...].astype(jnp.float32))


def call(kernel, outs, *args, scratch=(), **kw):
    return pl.pallas_call(
        kernel,
        out_shape=outs,
        in_specs=[pl.BlockSpec(memory_space=pltpu.VMEM)] * len(args),
        out_specs=jax.tree.map(lambda _: pl.BlockSpec(memory_space=pltpu.VMEM), outs),
        scratch_shapes=scratch,
        compiler_params=pltpu.CompilerParams(vmem_limit_bytes=24 << 20),
        name=kernel.__name__,
        **kw,
    )(*args)


def index(y, x, z):
    return ((y % 2) * 4 + x % 4) * 4 + z % 4


def shift(a, dy=0, dx=0, dz=0):
    pairs = [(index(y, x, z), index(y + dy, x + dx, z + dz)) for y in range(2) for x in range(4) for z in range(4)]
    return lax.ppermute(a, "col", pairs)


def swap(a, k):
    return lax.ppermute(a, "row", [(r, r ^ k) for r in range(4)])


def from_three(a, axis):
    return [shift(a, **{axis: -o}) for o in OFFSETS[1:]]


def body(row_coords, col_coords, start_block):
    f32 = jnp.float32
    mine = centred(row_coords).astype(jnp.bfloat16)
    other = shift(mine, dy=1)
    first = [jnp.concatenate([mine[:, h : h + 16], other[:, h : h + 16]], axis=1) for h in (0, 16)]
    line = [
        jnp.concatenate([first[0], *from_three(first[0], "dz")], axis=1),
        jnp.concatenate([first[1], *from_three(first[1], "dx")], axis=1),
    ]
    far0 = from_three(line[0], "dx")
    far1 = from_three(line[1], "dz")

    wide = centred(col_coords)
    cols = (wide * (4.0 / ATOMS)).astype(jnp.bfloat16)
    cn = (jnp.sum(wide * wide, axis=(0, 2)) * (2.0 / ATOMS)).reshape(-1, 1, TC)
    block_mean = jnp.mean(start_block, axis=0, keepdims=True)
    start = start_block - block_mean
    start_hi = lax.reduce_precision(start, 8, 7)
    sw = jnp.concatenate(
        [start_hi.astype(jnp.bfloat16), (start - start_hi).astype(jnp.bfloat16), jnp.ones((start.shape[0], 128), jnp.bfloat16)],
        axis=1,
    )
    bm = jnp.concatenate([block_mean, block_mean], axis=1)

    chunks = [
        dist_call(line, cols, cn, sw),
        dist_call([far0[0], far0[1], far1[0], far1[1]], cols, cn, sw),
        dist_call([far0[2], far1[2]], cols, cn, sw),
    ]
    n = lax.axis_size("col")
    packed = jax.ShapeDtypeStruct((n, 24, 128), f32)
    sent = call(pack_kernel, packed, *(c[2] for c in chunks), bm)
    got = lax.all_to_all(sent, "col", 0, 0, tiled=True)
    totals = call(owner_kernel, packed, got)
    got = lax.all_to_all(totals, "col", 0, 0, tiled=True)
    left, tc, stat = call(
        panel_kernel,
        (
            jax.ShapeDtypeStruct((144, 32 * n), jnp.bfloat16),
            jax.ShapeDtypeStruct((32 * n, K), f32),
            jax.ShapeDtypeStruct((72, 128), f32),
        ),
        got,
        scratch=[pltpu.VMEM((32 * n, 128), f32)],
    )
    stats = [stat, *(swap(stat, k) for k in (1, 2, 3))]
    me = lax.axis_index("row").reshape(1)
    partial = image_call(me, left, chunks)
    arrived = [partial[0:1], *(swap(partial[k : k + 1], k) for k in (1, 2, 3))]
    m, d = call(
        factor_kernel, (jax.ShapeDtypeStruct((64, 128), f32), jax.ShapeDtypeStruct((8, 128), f32)), *stats
    )
    part = call(join_kernel, jax.ShapeDtypeStruct((64, TC), jnp.bfloat16), *arrived, m, d)
    parts = [part, *(swap(part, k) for k in (1, 2, 3))]
    basis = call(basis_kernel, jax.ShapeDtypeStruct((32 * n, K), f32), tc, m, d)
    image = call(spread_kernel, jax.ShapeDtypeStruct((4 * TC, K), f32), *parts)
    return (basis, image)


def solution(mesh):
    in_specs = (P(None, ("row", "col"), None), P(None, "col", None), P("col", None))
    out_specs = (P("row", None), P("col", None))
    return jax.shard_map(body, mesh=mesh, in_specs=in_specs, out_specs=out_specs, check_vma=False)
```

```python
import functools

import jax
import jax.numpy as jnp
from jax import lax
from jax.experimental import pallas as pl
from jax.experimental.pallas import tpu as pltpu
from jax.sharding import PartitionSpec as P

ATOMS = 512
NEWTON = 8
K = 64
TR = 128
TC = 512
NC = 256
RF = 4096
CF = 32768
HIGHEST = lax.Precision.HIGHEST
OFFSETS = (0, -1, 1, 2)


def centred(coords):
    wide = coords.astype(jnp.float32)
    wide = wide - jnp.mean(wide, axis=2, keepdims=True)
    return lax.reduce_precision(wide, 8, 7)


def newton_slice(p, u):
    def g(i, j):
        return p[0][i] * p[0][j] + p[1][i] * p[1][j] + p[2][i] * p[2][j]

    g00, g11, g22, g01, g02, g12 = g(0, 0), g(1, 1), g(2, 2), g(0, 1), g(0, 2), g(1, 2)
    det = (
        p[0][0] * (p[1][1] * p[2][2] - p[1][2] * p[2][1])
        - p[0][1] * (p[1][0] * p[2][2] - p[1][2] * p[2][0])
        + p[0][2] * (p[1][0] * p[2][1] - p[1][1] * p[2][0])
    )
    q = g00 + g11 + g22
    cross = g01 * g01 + g02 * g02 + g12 * g12
    square = g00 * g00 + g11 * g11 + g22 * g22 + (cross + cross)
    half = 0.5 * q
    rest = half * half - 0.5 * square
    twice = det + det
    x = u
    for _ in range(NEWTON):
        s = x * x
        x = ((0.75 * s - half) * s + rest) / ((s - q) * x - twice)
    return u - x


def dist_kernel(ns, *refs):
    rows = refs[:ns]
    cols, cn, sw = refs[ns : ns + 3]
    hi, lo, t_out = refs[ns + 3 : ns + 6]
    bufs, rn = refs[ns + 6 : ns + 8], refs[ns + 8]
    nb = rn.shape[0]
    per = nb // ns
    ct = pl.program_id(0)
    last = pl.num_programs(0) - 1

    def frames(rb):
        r = (rb % per) * TR
        return rows[rb // per][:, r : r + TR, :]

    def products(rb, at, buf, units):
        c0 = pl.multiple_of(at * TC, TC)
        lhs = frames(rb).reshape(3 * TR, ATOMS)
        for b, n in units:
            buf[b, :, n * 256 : n * 256 + 256] = lax.dot_general(
                lhs, cols[b, pl.ds(c0 + n * 256, 256), :], (((1,), (1,)), ((), ())), preferred_element_type=jnp.float32
            )

    def newton(rb, buf, slices):
        for r, c in slices:
            p = [[buf[b, a * TR + r : a * TR + r + 16, c : c + 128] for b in range(3)] for a in range(3)]
            u = rn[rb, r : r + 16] + cn[0, 0:1, c : c + 128]
            d = newton_slice(p, u)
            h = d.astype(jnp.bfloat16)
            hi[rb * TR + r : rb * TR + r + 16, c : c + 128] = h
            lo[rb * TR + r : rb * TR + r + 16, c : c + 128] = (d - h.astype(jnp.float32)).astype(jnp.bfloat16)

    def panel(rb):
        at = slice(rb * TR, rb * TR + TR)
        w = sw[:, pl.ds(pl.multiple_of(ct * TC, TC), TC)]
        dims = (((1,), (1,)), ((), ()))
        t_out[at, :] += lax.dot_general(hi[at, :], w, dims, preferred_element_type=jnp.float32) + lax.dot_general(
            lo[at, :], w, dims, preferred_element_type=jnp.float32
        )

    units = [(b, n) for n in range(TC // 256) for b in range(3)]
    slices = [(r, c) for r in range(0, TR, 16) for c in range(0, TC, 128)]
    share = -(-len(slices) // len(units))

    @pl.when(ct == 0)
    def _():
        t_out[...] = jnp.zeros_like(t_out)
        for rb in range(nb):
            w = frames(rb).astype(jnp.float32)
            n = jnp.sum(jnp.sum(w * w, axis=0), axis=1, keepdims=True) * (2.0 * ATOMS / 16.0)
            rn[rb] = jnp.broadcast_to(n, (TR, 128))
        products(0, 0, bufs[0], units)

    for rb in range(nb):
        after, at = (rb + 1, ct) if rb + 1 < nb else (0, jnp.minimum(ct + 1, last))

        @pl.when(ct <= last)
        def _(rb=rb, after=after, at=at):
            for i in range(len(units)):
                newton(rb, bufs[rb % 2], slices[i * share : (i + 1) * share])
                products(after, at, bufs[(rb + 1) % 2], units[i : i + 1])
                if i == 2 and rb > 0:
                    panel(rb - 1)

    panel(nb - 1)


def whole(a):
    return pl.BlockSpec(a.shape, lambda *_: (0,) * a.ndim)


def dist_call(sources, cols, cn, sw):
    nc = cols.shape[1]
    r = sum(a.shape[1] for a in sources)
    return pl.pallas_call(
        functools.partial(dist_kernel, len(sources)),
        grid=(nc // TC,),
        in_specs=[whole(a) for a in sources]
        + [whole(cols), pl.BlockSpec((1, 1, TC), lambda c: (c, 0, 0)), whole(sw)],
        out_specs=[
            pl.BlockSpec((r, TC), lambda c: (0, c)),
            pl.BlockSpec((r, TC), lambda c: (0, c)),
            pl.BlockSpec((r, 256), lambda c: (0, 0)),
        ],
        out_shape=[
            jax.ShapeDtypeStruct((r, nc), jnp.bfloat16),
            jax.ShapeDtypeStruct((r, nc), jnp.bfloat16),
            jax.ShapeDtypeStruct((r, 256), jnp.float32),
        ],
        scratch_shapes=[
            pltpu.VMEM((3, 3 * TR, TC), jnp.float32),
            pltpu.VMEM((3, 3 * TR, TC), jnp.float32),
            pltpu.VMEM((r // TR, TR, 128), jnp.float32),
        ],
        compiler_params=pltpu.CompilerParams(dimension_semantics=("arbitrary",), vmem_limit_bytes=60 << 20),
        cost_estimate=pl.CostEstimate(
            flops=r * nc * 9 * 2 * ATOMS, bytes_accessed=8 << 20, transcendentals=r * nc * NEWTON
        ),
        name=f"dist{r}",
    )(*sources, cols, cn, sw)


PIECES = [(dy, i, o) for dy in range(2) for i in range(4) for o in range(4)]
CHUNK_OF = ((0, 0), (1, 0), (1, 256), (2, 0))
CHUNK_START = (0, 256, 768)


def place(dy, i, o):
    chunk, start = CHUNK_OF[o]
    return chunk, start + (i * 2 + dy) * 32


def owner_of(dy, i, o):
    me, core = lax.axis_index("col"), lax.axis_index("row") % 2
    y, x, z = me // 16, (me // 4) % 4, me % 4
    dx = OFFSETS[o] + core * (OFFSETS[i] - OFFSETS[o])
    dz = OFFSETS[i] + core * (OFFSETS[o] - OFFSETS[i])
    return ((y + dy) % 2) * 16 + ((x + dx + 4) % 4) * 4 + (z + dz + 4) % 4


def lanes(shape):
    return lax.broadcasted_iota(jnp.int32, shape, len(shape) - 1)


def pack_kernel(t0, t1, t2, bm, out):
    ts = (t0, t1, t2)
    lane16, lane8 = lanes((16, 128)), lanes((8, 128))
    means = jnp.broadcast_to(bm[...], (8, 128))
    for piece in PIECES:
        dest = owner_of(*piece)
        chunk, at = place(*piece)
        full, sums = [], []
        for r in (at, at + 16):
            t = ts[chunk][r : r + 16, 0:128]
            full.append(t + pltpu.roll(t, 64, 1))
            sums.append(ts[chunk][r : r + 16, 128:256])
        out[dest, 0:16, :] = jnp.where(lane16 < 64, full[0], full[1])
        ext = jnp.where(lane8 < 16, sums[0][0:8], sums[0][8:16])
        ext = jnp.where(lane8 < 32, ext, sums[1][0:8])
        ext = jnp.where(lane8 < 48, ext, sums[1][8:16])
        out[dest, 16:24, :] = jnp.where(lane8 < 64, ext, means)


def owner_kernel(got, out):
    lane = lanes((8, 128))

    def spread(ext):
        one = lambda k: jnp.broadcast_to(ext[:, k : k + 1], (8, 128))
        return jnp.where(lane < 64, one(0), one(32)), jnp.where(lane < 64, one(16), one(48))

    zero = jnp.zeros((8, 128), jnp.float32)
    a, b, e = zero, zero, zero
    for src in range(got.shape[0]):
        ext = got[src, 16:24, :]
        bm = jnp.where(lane < 64, pltpu.roll(ext, 64, 1), ext)
        r0, r1 = spread(ext)
        a = a + (got[src, 0:8, :] + r0 * bm)
        b = b + (got[src, 8:16, :] + r1 * bm)
        e = e + ext
    bm = jnp.where(lane < 64, pltpu.roll(e, 64, 1), e) * (1.0 / got.shape[0])
    r0, r1 = spread(e)
    a = a - r0 * bm
    b = b - r1 * bm
    sub = lax.broadcasted_iota(jnp.int32, (8, 128), 0)
    y = jnp.sum(r0 * a + r1 * b, axis=0, keepdims=True)
    tot = jnp.sum(r0 + r1, axis=0, keepdims=True)
    ext = jnp.where(sub == 0, jnp.broadcast_to(y, (8, 128)), jnp.broadcast_to(tot, (8, 128)))
    for dst in range(got.shape[0]):
        out[dst, 0:8, :] = a
        out[dst, 8:16, :] = b
        out[dst, 16:24, :] = ext


def panel_kernel(got, left, tc_out, stat, arr):
    n = got.shape[0]
    lane1 = lanes((1, 128))

    def both(v):
        return v + pltpu.roll(v, 64, 1)

    total = jnp.sum(jnp.sum(got[:, 0:16, :], axis=0), axis=0, keepdims=True)
    mean = both(total) * (1.0 / (32 * n))
    ext = jnp.sum(got[:, 16:24, :], axis=0)
    y, rows = both(ext[0:1]), both(ext[1:2])
    x = got[:, 0:16, :] - mean
    flat = x.reshape(n * 16, 128)
    g = lax.dot_general(flat, flat, (((0,), (0,)), ((), ())), precision=HIGHEST, preferred_element_type=jnp.float32)
    stat[0:64, :] = g[0:64, :] + pltpu.roll(g[64:128, :], 64, 1)
    sub = lax.broadcasted_iota(jnp.int32, (8, 128), 0)
    tile = jnp.where(sub == 0, mean, jnp.where(sub == 1, y, rows))
    stat[64:72, :] = jnp.broadcast_to(tile, (8, 128))
    for b in range(n):
        tc_out[b * 32 : b * 32 + 16, :] = x[b, :, 0:64]
        tc_out[b * 32 + 16 : b * 32 + 32, :] = x[b, :, 64:128]
    for piece in PIECES:
        src = owner_of(*piece)
        t = got[src, 0:16, :] - mean
        chunk, r = place(*piece)
        r += CHUNK_START[chunk]
        arr[r : r + 16, :] = t
        arr[r + 16 : r + 32, :] = pltpu.roll(t, 64, 1)
    pt = jnp.transpose(arr[...])[0:64, :]
    h = pt.astype(jnp.bfloat16)
    left[0:64, :] = h
    left[64:128, :] = (pt - h.astype(jnp.float32)).astype(jnp.bfloat16)
    left[128:144, :] = jnp.ones((16, pt.shape[1]), jnp.bfloat16)


def image_kernel(me, left, h0, l0, h1, l1, h2, l2, out):
    acc = jnp.zeros((144, NC), jnp.float32)
    for at, refs in ((0, (h0, l0)), (256, (h1, l1)), (768, (h2, l2))):
        for ref in refs:
            acc += jnp.dot(left[:, at : at + ref.shape[0]], ref[...], preferred_element_type=jnp.float32)
    out[0, 0:64, :] = acc[0:64] + acc[64:128]
    out[0, 64:72, :] = acc[128:136]


def image_call(me, left, chunks):
    flat = [a for c in chunks for a in c[:2]]
    spec = lambda a: pl.BlockSpec((a.shape[0], NC), lambda k, me: (0, me[0] ^ k))
    return pl.pallas_call(
        image_kernel,
        grid_spec=pltpu.PrefetchScalarGridSpec(
            num_scalar_prefetch=1,
            grid=(4,),
            in_specs=[pl.BlockSpec(left.shape, lambda k, me: (0, 0))] + [spec(a) for a in flat],
            out_specs=pl.BlockSpec((1, 72, NC), lambda k, me: (k, 0, 0)),
        ),
        out_shape=jax.ShapeDtypeStruct((4, 72, NC), jnp.float32),
        compiler_params=pltpu.CompilerParams(dimension_semantics=("arbitrary",), vmem_limit_bytes=60 << 20),
        cost_estimate=pl.CostEstimate(flops=2 * 2 * 256 * 1024 * 1024, bytes_accessed=5 << 20, transcendentals=0),
        name="image",
    )(me, left, *flat)


def factor_kernel(s0, s1, s2, s3, m_out, d_out):
    stats = (s0, s1, s2, s3)

    def total(lo, hi):
        return (s0[lo:hi, :] + s1[lo:hi, :]) + (s2[lo:hi, :] + s3[lo:hi, :])

    mean = total(64, 65) * 0.25
    offs = [s[64:65, :] - mean for s in stats]
    y = total(65, 66) - mean * total(66, 67)
    sub = lax.broadcasted_iota(jnp.int32, (8, 128), 0)
    deltas = jnp.zeros((8, 128), jnp.float32)
    for k in range(4):
        deltas = jnp.where(sub == k, offs[k], deltas)
    d_out[...] = jnp.where(sub == 4, y * (1.0 / CF), deltas)
    outer = lax.dot_general(
        deltas, deltas, (((0,), (0,)), ((), ())), precision=HIGHEST, preferred_element_type=jnp.float32
    )
    gram = (total(0, 64) + outer[0:64, :] * (RF // 4)) * (1.0 / (16 * RF))
    lane = lanes((64, 128))
    row = lax.broadcasted_iota(jnp.int32, (64, 128), 0)
    a = jnp.where(lane < 64, gram, jnp.where(lane - 64 == row, 1.0, 0.0))
    for k in range(0, 64, 2):
        r0, r1 = a[k : k + 1, :], a[k + 1 : k + 2, :]
        p, q, s = r0[:, k : k + 1], r0[:, k + 1 : k + 2], r1[:, k + 1 : k + 2]
        inv = 1.0 / (p * s - q * q)
        y0, y1 = (s * r0 - q * r1) * inv, (p * r1 - q * r0) * inv
        c0 = jnp.where(row > k + 1, a[:, k : k + 1], 0.0)
        c1 = jnp.where(row > k + 1, a[:, k + 1 : k + 2], 0.0)
        a = a - (c0 * y0 + c1 * y1)
        tilt = q / p
        m_out[k : k + 1, :] = r0 * (lax.rsqrt(p) * -0.25)
        m_out[k + 1 : k + 2, :] = (r1 - tilt * r0) * (lax.rsqrt(s - tilt * q) * -0.25)


def join_kernel(w, g1, g2, g3, m, d, out):
    parts = ((w[0, 0:64] + g1[0, 0:64]) + (g2[0, 0:64] + g3[0, 0:64]))
    sub = lax.broadcasted_iota(jnp.int32, (8, NC), 0)
    sums = jnp.where(sub == 4, -1.0, 0.0)
    for k, ref in enumerate((w, g1, g2, g3)):
        sums = jnp.where(sub == k, ref[0, 64:72], sums)
    add = lax.dot_general(
        d[...], sums, (((0,), (0,)), ((), ())), precision=HIGHEST, preferred_element_type=jnp.float32
    )
    inv = pltpu.roll(m[...], 64, 1)[:, 0:64]
    res = jnp.dot(inv, parts + add[0:64], precision=HIGHEST, preferred_element_type=jnp.float32)
    out[...] = (res * (-0.25 / RF**0.5)).astype(jnp.bfloat16)


def basis_kernel(tc, m, d, out):
    inv = pltpu.roll(m[...], 64, 1)[:, 0:64]
    x = tc[...] + d[0:1, 0:64]
    out[...] = lax.dot_general(
        inv, x, (((1,), (1,)), ((), ())), precision=HIGHEST, preferred_element_type=jnp.float32
    )


def spread_kernel(i0, i1, i2, i3, out):
    me = lax.axis_index("row")
    for k, ref in enumerate((i0, i1, i2, i3)):
        at = pl.multiple_of((me ^ k) * NC, NC)
        out[:, pl.ds(at, NC)] = ref[...].astype(jnp.float32)


def call(kernel, outs, *args, scratch=(), **kw):
    return pl.pallas_call(
        kernel,
        out_shape=outs,
        in_specs=[pl.BlockSpec(memory_space=pltpu.VMEM)] * len(args),
        out_specs=jax.tree.map(lambda _: pl.BlockSpec(memory_space=pltpu.VMEM), outs),
        scratch_shapes=scratch,
        compiler_params=pltpu.CompilerParams(vmem_limit_bytes=24 << 20),
        name=kernel.__name__,
        **kw,
    )(*args)


def index(core, lo, y, x, z):
    return (lo * 2 + core) * 32 + ((y % 2) * 4 + x % 4) * 4 + z % 4


DEVICES = [(c, w, y, x, z) for c in range(2) for w in range(2) for y in range(2) for x in range(4) for z in range(4)]


def shift(a, dy=0, inner=0, outer=0):
    pairs = []
    for c, w, y, x, z in DEVICES:
        dx, dz = (inner, outer) if c else (outer, inner)
        pairs.append((index(c, w, y, x, z), index(c, w, y + dy, x + dx, z + dz)))
    return lax.ppermute(a, ("row", "col"), pairs)


def swap(a, k):
    return lax.ppermute(a, "row", [(r, r ^ k) for r in range(4)])


def from_three(a, axis):
    return [shift(a, **{axis: -o}) for o in OFFSETS[1:]]


def body(row_coords, col_coords, start_block):
    f32 = jnp.float32
    mine = (centred(row_coords) * (4.0 / ATOMS)).astype(jnp.bfloat16)
    pair = jnp.concatenate([mine, shift(mine, dy=1)], axis=1)
    line = jnp.concatenate([pair, *from_three(pair, "inner")], axis=1)
    far = from_three(line, "outer")

    wide = centred(col_coords)
    cols = wide.astype(jnp.bfloat16)
    cn = (jnp.sum(wide * wide, axis=(0, 2)) * (2.0 / ATOMS)).reshape(-1, 1, TC)
    start = start_block.T
    block_mean = jnp.mean(start, axis=1)
    start = start - block_mean[:, None]
    start_hi = lax.reduce_precision(start, 8, 7)
    ones = jnp.ones((128, start.shape[1]), jnp.bfloat16)
    sw = jnp.concatenate([start_hi.astype(jnp.bfloat16), (start - start_hi).astype(jnp.bfloat16), ones], axis=0)
    bm = jnp.concatenate([block_mean, block_mean])[None, :]

    chunks = [dist_call([line], cols, cn, sw), dist_call(far[:2], cols, cn, sw), dist_call(far[2:], cols, cn, sw)]
    n = lax.axis_size("col")
    packed = jax.ShapeDtypeStruct((n, 24, 128), f32)
    sent = call(pack_kernel, packed, *(c[2] for c in chunks), bm)
    got = lax.all_to_all(sent, "col", 0, 0, tiled=True)
    totals = call(owner_kernel, packed, got)
    got = lax.all_to_all(totals, "col", 0, 0, tiled=True)
    left, tc, stat = call(
        panel_kernel,
        (
            jax.ShapeDtypeStruct((144, 32 * n), jnp.bfloat16),
            jax.ShapeDtypeStruct((32 * n, K), f32),
            jax.ShapeDtypeStruct((72, 128), f32),
        ),
        got,
        scratch=[pltpu.VMEM((32 * n, 128), f32)],
    )
    stats = [stat, *(swap(stat, k) for k in (1, 2, 3))]
    me = lax.axis_index("row").reshape(1)
    partial = image_call(me, left, chunks)
    arrived = [partial[0:1], *(swap(partial[k : k + 1], k) for k in (1, 2, 3))]
    m, d = call(
        factor_kernel, (jax.ShapeDtypeStruct((64, 128), f32), jax.ShapeDtypeStruct((8, 128), f32)), *stats
    )
    part = call(join_kernel, jax.ShapeDtypeStruct((64, NC), jnp.bfloat16), *arrived, m, d)
    parts = [part, *(swap(part, k) for k in (1, 2, 3))]
    basis = call(basis_kernel, jax.ShapeDtypeStruct((K, 32 * n), f32), tc, m, d)
    image = call(spread_kernel, jax.ShapeDtypeStruct((K, 4 * NC), f32), *parts)
    return (basis.T, image.T)


def solution(mesh):
    in_specs = (P(None, ("row", "col"), None), P(None, "col", None), P("col", None))
    out_specs = (P("row", None), P("col", None))
    return jax.shard_map(body, mesh=mesh, in_specs=in_specs, out_specs=out_specs, check_vma=False)
```

```python
import functools

import jax
import jax.numpy as jnp
from jax import lax
from jax.experimental import pallas as pl
from jax.experimental.pallas import tpu as pltpu
from jax.sharding import PartitionSpec as P

ATOMS = 512
NEWTON = 8
K = 64
TR = 128
TC = 512
NC = 256
RF = 4096
CF = 32768
HIGHEST = lax.Precision.HIGHEST
OFFSETS = (0, -1, 1, 2)


def centred(coords):
    wide = coords.astype(jnp.float32)
    wide = wide - jnp.mean(wide, axis=2, keepdims=True)
    return lax.reduce_precision(wide, 8, 7)


def newton_slice(p, u):
    def g(i, j):
        return p[0][i] * p[0][j] + p[1][i] * p[1][j] + p[2][i] * p[2][j]

    g00, g11, g22, g01, g02, g12 = g(0, 0), g(1, 1), g(2, 2), g(0, 1), g(0, 2), g(1, 2)
    det = (
        p[0][0] * (p[1][1] * p[2][2] - p[1][2] * p[2][1])
        - p[0][1] * (p[1][0] * p[2][2] - p[1][2] * p[2][0])
        + p[0][2] * (p[1][0] * p[2][1] - p[1][1] * p[2][0])
    )
    q = g00 + g11 + g22
    cross = g01 * g01 + g02 * g02 + g12 * g12
    square = g00 * g00 + g11 * g11 + g22 * g22 + (cross + cross)
    half = 0.5 * q
    rest = half * half - 0.5 * square
    twice = det + det
    x = u
    for _ in range(NEWTON):
        s = x * x
        x = ((0.75 * s - half) * s + rest) / ((s - q) * x - twice)
    return u - x


def dist_kernel(ns, *refs):
    rows = refs[:ns]
    cols, cn, sw = refs[ns : ns + 3]
    outs, t_out = refs[ns + 3 : ns + 5], refs[ns + 5]
    bufs, rn, kept, sems = refs[ns + 6 : ns + 8], refs[ns + 8], refs[ns + 9 : ns + 11], refs[ns + 11]
    nb = rn.shape[0]
    per = nb // ns
    ct = pl.program_id(0)
    last = pl.num_programs(0) - 1

    def frames(rb):
        r = (rb % per) * TR
        return rows[rb // per][:, r : r + TR, :]

    def products(rb, at, buf, units):
        c0 = pl.multiple_of(at * TC, TC)
        lhs = frames(rb).reshape(3 * TR, ATOMS)
        for b, n in units:
            buf[b, :, n * 256 : n * 256 + 256] = lax.dot_general(
                lhs, cols[b, pl.ds(c0 + n * 256, 256), :], (((1,), (1,)), ((), ())), preferred_element_type=jnp.float32
            )

    def newton(rb, buf, slices):
        for r, c in slices:
            p = [[buf[b, a * TR + r : a * TR + r + 16, c : c + 128] for b in range(3)] for a in range(3)]
            u = rn[rb, r : r + 16] + cn[0, 0:1, c : c + 128]
            d = newton_slice(p, u)
            h = d.astype(jnp.bfloat16)
            kept[0][ct, rb * TR + r : rb * TR + r + 16, c : c + 128] = h
            kept[1][ct, rb * TR + r : rb * TR + r + 16, c : c + 128] = (d - h.astype(jnp.float32)).astype(jnp.bfloat16)

    def stores(at, rb):
        rows_at = pl.ds(rb * TR, TR)
        return [
            pltpu.make_async_copy(
                kept[i].at[at, rows_at, :], outs[i].at[rows_at, pl.ds(pl.multiple_of(at * TC, TC), TC)], sems.at[i, at, rb]
            )
            for i in range(2)
        ]

    def panel(rb):
        at = slice(rb * TR, rb * TR + TR)
        w = sw[:, pl.ds(pl.multiple_of(ct * TC, TC), TC)]
        dims = (((1,), (1,)), ((), ()))
        t_out[at, :] += lax.dot_general(
            kept[0][ct, at, :], w, dims, preferred_element_type=jnp.float32
        ) + lax.dot_general(kept[1][ct, at, :], w, dims, preferred_element_type=jnp.float32)

    units = [(b, n) for n in range(TC // 256) for b in range(3)]
    slices = [(r, c) for r in range(0, TR, 16) for c in range(0, TC, 128)]
    share = -(-len(slices) // len(units))

    @pl.when(ct == 0)
    def _():
        t_out[...] = jnp.zeros_like(t_out)
        for rb in range(nb):
            w = frames(rb).astype(jnp.float32)
            n = jnp.sum(jnp.sum(w * w, axis=0), axis=1, keepdims=True) * (2.0 * ATOMS / 16.0)
            rn[rb] = jnp.broadcast_to(n, (TR, 128))
        products(0, 0, bufs[0], units)

    for rb in range(nb):
        after, at = (rb + 1, ct) if rb + 1 < nb else (0, jnp.minimum(ct + 1, last))

        @pl.when(ct <= last)
        def _(rb=rb, after=after, at=at):
            for i in range(len(units)):
                newton(rb, bufs[rb % 2], slices[i * share : (i + 1) * share])
                products(after, at, bufs[(rb + 1) % 2], units[i : i + 1])
                if i == 2 and rb > 0:
                    panel(rb - 1)

        for copy in stores(ct, rb):
            copy.start()

    panel(nb - 1)

    @pl.when(ct == last)
    def _():
        for at in range(sems.shape[1]):
            for rb in range(nb):
                for copy in stores(at, rb):
                    copy.wait()


def whole(a):
    return pl.BlockSpec(a.shape, lambda *_: (0,) * a.ndim)


def dist_call(sources, cols, cn, sw):
    nc = cols.shape[1]
    r = sum(a.shape[1] for a in sources)
    return pl.pallas_call(
        functools.partial(dist_kernel, len(sources)),
        grid=(nc // TC,),
        in_specs=[whole(a) for a in sources]
        + [whole(cols), pl.BlockSpec((1, 1, TC), lambda c: (c, 0, 0)), whole(sw)],
        out_specs=[
            pl.BlockSpec(memory_space=pltpu.HBM),
            pl.BlockSpec(memory_space=pltpu.HBM),
            pl.BlockSpec((r, 256), lambda c: (0, 0)),
        ],
        out_shape=[
            pltpu.HBM((r, nc), jnp.bfloat16),
            pltpu.HBM((r, nc), jnp.bfloat16),
            jax.ShapeDtypeStruct((r, 256), jnp.float32),
        ],
        scratch_shapes=[
            pltpu.VMEM((3, 3 * TR, TC), jnp.float32),
            pltpu.VMEM((3, 3 * TR, TC), jnp.float32),
            pltpu.VMEM((r // TR, TR, 128), jnp.float32),
            pltpu.VMEM((nc // TC, r, TC), jnp.bfloat16),
            pltpu.VMEM((nc // TC, r, TC), jnp.bfloat16),
            pltpu.SemaphoreType.DMA((2, nc // TC, r // TR)),
        ],
        compiler_params=pltpu.CompilerParams(dimension_semantics=("arbitrary",), vmem_limit_bytes=20 << 20),
        cost_estimate=pl.CostEstimate(
            flops=r * nc * 9 * 2 * ATOMS, bytes_accessed=8 << 20, transcendentals=r * nc * NEWTON
        ),
        name=f"dist{r}",
    )(*sources, cols, cn, sw)


PIECES = [(dy, i, o) for dy in range(2) for i in range(4) for o in range(4)]
CHUNK_START = (0, 256, 512, 768)


def place(dy, i, o):
    return o, (i * 2 + dy) * 32


def owner_of(dy, i, o):
    me, core = lax.axis_index("col"), lax.axis_index("row") % 2
    y, x, z = me // 16, (me // 4) % 4, me % 4
    dx = OFFSETS[o] + core * (OFFSETS[i] - OFFSETS[o])
    dz = OFFSETS[i] + core * (OFFSETS[o] - OFFSETS[i])
    return ((y + dy) % 2) * 16 + ((x + dx + 4) % 4) * 4 + (z + dz + 4) % 4


def lanes(shape):
    return lax.broadcasted_iota(jnp.int32, shape, len(shape) - 1)


def pack_kernel(t0, t1, t2, t3, bm, out):
    ts = (t0, t1, t2, t3)
    lane16, lane8 = lanes((16, 128)), lanes((8, 128))
    means = jnp.broadcast_to(bm[...], (8, 128))
    for piece in PIECES:
        dest = owner_of(*piece)
        chunk, at = place(*piece)
        full, sums = [], []
        for r in (at, at + 16):
            t = ts[chunk][r : r + 16, 0:128]
            full.append(t + pltpu.roll(t, 64, 1))
            sums.append(ts[chunk][r : r + 16, 128:256])
        out[dest, 0:16, :] = jnp.where(lane16 < 64, full[0], full[1])
        ext = jnp.where(lane8 < 16, sums[0][0:8], sums[0][8:16])
        ext = jnp.where(lane8 < 32, ext, sums[1][0:8])
        ext = jnp.where(lane8 < 48, ext, sums[1][8:16])
        out[dest, 16:24, :] = jnp.where(lane8 < 64, ext, means)


def owner_kernel(got, out):
    lane = lanes((8, 128))

    def spread(ext):
        one = lambda k: jnp.broadcast_to(ext[:, k : k + 1], (8, 128))
        return jnp.where(lane < 64, one(0), one(32)), jnp.where(lane < 64, one(16), one(48))

    zero = jnp.zeros((8, 128), jnp.float32)
    a, b, e = zero, zero, zero
    for src in range(got.shape[0]):
        ext = got[src, 16:24, :]
        bm = jnp.where(lane < 64, pltpu.roll(ext, 64, 1), ext)
        r0, r1 = spread(ext)
        a = a + (got[src, 0:8, :] + r0 * bm)
        b = b + (got[src, 8:16, :] + r1 * bm)
        e = e + ext
    bm = jnp.where(lane < 64, pltpu.roll(e, 64, 1), e) * (1.0 / got.shape[0])
    r0, r1 = spread(e)
    a = a - r0 * bm
    b = b - r1 * bm
    sub = lax.broadcasted_iota(jnp.int32, (8, 128), 0)
    y = jnp.sum(r0 * a + r1 * b, axis=0, keepdims=True)
    tot = jnp.sum(r0 + r1, axis=0, keepdims=True)
    ext = jnp.where(sub == 0, jnp.broadcast_to(y, (8, 128)), jnp.broadcast_to(tot, (8, 128)))
    for dst in range(got.shape[0]):
        out[dst, 0:8, :] = a
        out[dst, 8:16, :] = b
        out[dst, 16:24, :] = ext


def panel_kernel(got, left, tc_out, stat, arr):
    n = got.shape[0]
    lane1 = lanes((1, 128))

    def both(v):
        return v + pltpu.roll(v, 64, 1)

    total = jnp.sum(jnp.sum(got[:, 0:16, :], axis=0), axis=0, keepdims=True)
    mean = both(total) * (1.0 / (32 * n))
    ext = jnp.sum(got[:, 16:24, :], axis=0)
    y, rows = both(ext[0:1]), both(ext[1:2])
    x = got[:, 0:16, :] - mean
    flat = x.reshape(n * 16, 128)
    g = lax.dot_general(flat, flat, (((0,), (0,)), ((), ())), precision=HIGHEST, preferred_element_type=jnp.float32)
    stat[0:64, :] = g[0:64, :] + pltpu.roll(g[64:128, :], 64, 1)
    sub = lax.broadcasted_iota(jnp.int32, (8, 128), 0)
    tile = jnp.where(sub == 0, mean, jnp.where(sub == 1, y, rows))
    stat[64:72, :] = jnp.broadcast_to(tile, (8, 128))
    for b in range(n):
        tc_out[b * 32 : b * 32 + 16, :] = x[b, :, 0:64]
        tc_out[b * 32 + 16 : b * 32 + 32, :] = x[b, :, 64:128]
    for piece in PIECES:
        src = owner_of(*piece)
        t = got[src, 0:16, :] - mean
        chunk, r = place(*piece)
        r += CHUNK_START[chunk]
        arr[r : r + 16, :] = t
        arr[r + 16 : r + 32, :] = pltpu.roll(t, 64, 1)
    pt = jnp.transpose(arr[...])[0:64, :]
    h = pt.astype(jnp.bfloat16)
    left[0:64, :] = h
    left[64:128, :] = (pt - h.astype(jnp.float32)).astype(jnp.bfloat16)
    left[128:144, :] = jnp.ones((16, pt.shape[1]), jnp.bfloat16)


def image_kernel(me, left, h0, l0, h1, l1, h2, l2, h3, l3, *outs):
    acc = jnp.zeros((144, NC), jnp.float32)
    for at, refs in zip(CHUNK_START, ((h0, l0), (h1, l1), (h2, l2), (h3, l3))):
        for ref in refs:
            acc += jnp.dot(left[:, at : at + ref.shape[0]], ref[...], preferred_element_type=jnp.float32)
    for k in range(4):

        @pl.when(pl.program_id(0) == k)
        def _(k=k):
            outs[k][0:64, :] = acc[0:64] + acc[64:128]
            outs[k][64:72, :] = acc[128:136]


def image_call(me, left, chunks):
    flat = [a for c in chunks for a in c[:2]]
    spec = lambda a: pl.BlockSpec((a.shape[0], NC), lambda k, me: (0, me[0] ^ k))
    return pl.pallas_call(
        image_kernel,
        grid_spec=pltpu.PrefetchScalarGridSpec(
            num_scalar_prefetch=1,
            grid=(4,),
            in_specs=[pl.BlockSpec(left.shape, lambda k, me: (0, 0))] + [spec(a) for a in flat],
            out_specs=[pl.BlockSpec((72, NC), lambda k, me: (0, 0))] * 4,
        ),
        out_shape=[jax.ShapeDtypeStruct((72, NC), jnp.float32)] * 4,
        compiler_params=pltpu.CompilerParams(dimension_semantics=("arbitrary",), vmem_limit_bytes=16 << 20),
        cost_estimate=pl.CostEstimate(flops=2 * 2 * 256 * 1024 * 1024, bytes_accessed=5 << 20, transcendentals=0),
        name="image",
    )(me, left, *flat)


def factor_kernel(s0, s1, s2, s3, m_out, d_out):
    stats = (s0, s1, s2, s3)

    def total(lo, hi):
        return (s0[lo:hi, :] + s1[lo:hi, :]) + (s2[lo:hi, :] + s3[lo:hi, :])

    mean = total(64, 65) * 0.25
    offs = [s[64:65, :] - mean for s in stats]
    y = total(65, 66) - mean * total(66, 67)
    sub = lax.broadcasted_iota(jnp.int32, (8, 128), 0)
    deltas = jnp.zeros((8, 128), jnp.float32)
    for k in range(4):
        deltas = jnp.where(sub == k, offs[k], deltas)
    d_out[...] = jnp.where(sub == 4, y * (1.0 / CF), deltas)
    outer = lax.dot_general(
        deltas, deltas, (((0,), (0,)), ((), ())), precision=HIGHEST, preferred_element_type=jnp.float32
    )
    gram = (total(0, 64) + outer[0:64, :] * (RF // 4)) * (1.0 / (16 * RF))
    lane = lanes((64, 128))
    row = lax.broadcasted_iota(jnp.int32, (64, 128), 0)
    a = jnp.where(lane < 64, gram, jnp.where(lane - 64 == row, 1.0, 0.0))
    tiles = [a[8 * t : 8 * t + 8, :] for t in range(8)]
    eighth = lax.broadcasted_iota(jnp.int32, (8, 128), 0)
    for t in range(8):
        cols = [[jnp.broadcast_to(tiles[i][:, 8 * t + j : 8 * t + j + 1], (8, 128)) for i in range(t, 8)] for j in range(8)]
        rest = tiles[t:]
        for j in range(8):
            spread = lambda v: jnp.broadcast_to(v[j : j + 1, :], (8, 128))
            pivot = spread(cols[j][0])
            inv = 1.0 / pivot
            row_j = spread(rest[0])
            m_out[8 * t + j : 8 * t + j + 1, :] = (row_j * (lax.rsqrt(pivot) * -0.25))[0:1, :]
            below = [v * inv for v in cols[j]]
            below[0] = jnp.where(eighth > j, below[0], 0.0)
            for l in range(j + 1, 8):
                top = spread(cols[l][0])
                cols[l] = [v - m * top for v, m in zip(cols[l], below)]
            rest = [v - m * row_j for v, m in zip(rest, below)]
        tiles[t:] = rest


def join_kernel(w, g1, g2, g3, m, d, out):
    parts = (w[0:64] + g1[0:64]) + (g2[0:64] + g3[0:64])
    sub = lax.broadcasted_iota(jnp.int32, (8, NC), 0)
    sums = jnp.where(sub == 4, -1.0, 0.0)
    for k, ref in enumerate((w, g1, g2, g3)):
        sums = jnp.where(sub == k, ref[64:72], sums)
    add = lax.dot_general(
        d[...], sums, (((0,), (0,)), ((), ())), precision=HIGHEST, preferred_element_type=jnp.float32
    )
    inv = pltpu.roll(m[...], 64, 1)[:, 0:64]
    res = jnp.dot(inv, parts + add[0:64], precision=HIGHEST, preferred_element_type=jnp.float32)
    out[...] = (res * (-0.25 / RF**0.5)).astype(jnp.bfloat16)


def basis_kernel(tc, m, d, out):
    inv = pltpu.roll(m[...], 64, 1)[:, 0:64]
    x = tc[...] + d[0:1, 0:64]
    out[...] = lax.dot_general(
        inv, x, (((1,), (1,)), ((), ())), precision=HIGHEST, preferred_element_type=jnp.float32
    )


def spread_kernel(i0, i1, i2, i3, out):
    me = lax.axis_index("row")
    for k, ref in enumerate((i0, i1, i2, i3)):
        at = pl.multiple_of((me ^ k) * NC, NC)
        out[:, pl.ds(at, NC)] = ref[...].astype(jnp.float32)


def call(kernel, outs, *args, scratch=(), **kw):
    return pl.pallas_call(
        kernel,
        out_shape=outs,
        in_specs=[pl.BlockSpec(memory_space=pltpu.VMEM)] * len(args),
        out_specs=jax.tree.map(lambda _: pl.BlockSpec(memory_space=pltpu.VMEM), outs),
        scratch_shapes=scratch,
        compiler_params=pltpu.CompilerParams(vmem_limit_bytes=24 << 20),
        name=kernel.__name__,
        **kw,
    )(*args)


def index(core, lo, y, x, z):
    return (lo * 2 + core) * 32 + ((y % 2) * 4 + x % 4) * 4 + z % 4


DEVICES = [(c, w, y, x, z) for c in range(2) for w in range(2) for y in range(2) for x in range(4) for z in range(4)]


def shift(a, dy=0, inner=0, outer=0):
    pairs = []
    for c, w, y, x, z in DEVICES:
        dx, dz = (inner, outer) if c else (outer, inner)
        pairs.append((index(c, w, y, x, z), index(c, w, y + dy, x + dx, z + dz)))
    return lax.ppermute(a, ("row", "col"), pairs)


def swap(a, k):
    return lax.ppermute(a, "row", [(r, r ^ k) for r in range(4)])


def from_three(a, axis):
    return [shift(a, **{axis: -o}) for o in OFFSETS[1:]]


def body(row_coords, col_coords, start_block):
    f32 = jnp.float32
    mine = (centred(row_coords) * (4.0 / ATOMS)).astype(jnp.bfloat16)
    pair = jnp.concatenate([mine, shift(mine, dy=1)], axis=1)
    line = jnp.concatenate([pair, *from_three(pair, "inner")], axis=1)
    far = from_three(line, "outer")

    wide = centred(col_coords)
    cols = wide.astype(jnp.bfloat16)
    cn = (jnp.sum(wide * wide, axis=(0, 2)) * (2.0 / ATOMS)).reshape(-1, 1, TC)
    start = start_block.T
    block_mean = jnp.mean(start, axis=1)
    start = start - block_mean[:, None]
    start_hi = lax.reduce_precision(start, 8, 7)
    ones = jnp.ones((128, start.shape[1]), jnp.bfloat16)
    sw = jnp.concatenate([start_hi.astype(jnp.bfloat16), (start - start_hi).astype(jnp.bfloat16), ones], axis=0)
    bm = jnp.concatenate([block_mean, block_mean])[None, :]

    chunks = [dist_call([rows], cols, cn, sw) for rows in (line, *far)]
    n = lax.axis_size("col")
    packed = jax.ShapeDtypeStruct((n, 24, 128), f32)
    sent = call(pack_kernel, packed, *(c[2] for c in chunks), bm)
    got = lax.all_to_all(sent, "col", 0, 0, tiled=True)
    totals = call(owner_kernel, packed, got)
    got = lax.all_to_all(totals, "col", 0, 0, tiled=True)
    left, tc, stat = call(
        panel_kernel,
        (
            jax.ShapeDtypeStruct((144, 32 * n), jnp.bfloat16),
            jax.ShapeDtypeStruct((32 * n, K), f32),
            jax.ShapeDtypeStruct((72, 128), f32),
        ),
        got,
        scratch=[pltpu.VMEM((32 * n, 128), f32)],
    )
    stats = [stat, *(swap(stat, k) for k in (1, 2, 3))]
    me = lax.axis_index("row").reshape(1)
    partial = image_call(me, left, chunks)
    arrived = [partial[0], *(swap(partial[k], k) for k in (1, 2, 3))]
    m, d = call(
        factor_kernel, (jax.ShapeDtypeStruct((64, 128), f32), jax.ShapeDtypeStruct((8, 128), f32)), *stats
    )
    part = call(join_kernel, jax.ShapeDtypeStruct((64, NC), jnp.bfloat16), *arrived, m, d)
    parts = [part, *(swap(part, k) for k in (1, 2, 3))]
    basis = call(basis_kernel, jax.ShapeDtypeStruct((K, 32 * n), f32), tc, m, d)
    image = call(spread_kernel, jax.ShapeDtypeStruct((K, 4 * NC), f32), *parts)
    return (basis.T, image.T)


def solution(mesh):
    in_specs = (P(None, ("row", "col"), None), P(None, "col", None), P("col", None))
    out_specs = (P("row", None), P("col", None))
    return jax.shard_map(body, mesh=mesh, in_specs=in_specs, out_specs=out_specs, check_vma=False)
```

```python
import functools

import jax
import jax.numpy as jnp
from jax import lax
from jax.experimental import pallas as pl
from jax.experimental.pallas import tpu as pltpu
from jax.sharding import PartitionSpec as P


ATOMS = 512
NEWTON = 8
K = 64
TR = 128
TC = 512
NC = 256
RF = 4096
CF = 32768
HIGHEST = lax.Precision.HIGHEST
OFFSETS = (0, -1, 1, 2)


def centred(coords):
    wide = coords.astype(jnp.float32)
    return wide - jnp.sum(wide, axis=-1, keepdims=True) * (1.0 / ATOMS)


def column_kernel(coords, out, norm):
    total = None
    for k in range(3):
        c = centred(coords[k]).astype(jnp.bfloat16)
        out[k] = c
        w = c.astype(jnp.float32)
        part = jnp.sum(w * w, axis=1, keepdims=True)
        total = part if total is None else total + part
    spread = jnp.broadcast_to(total * (2.0 / ATOMS), (total.shape[0], 128))
    norm[...] = jnp.transpose(spread)[0:8, :]


def column_call(coords):
    frames, step = coords.shape[1], 256
    block = pl.BlockSpec((3, step, ATOMS), lambda i: (0, i, 0))
    return pl.pallas_call(
        column_kernel,
        grid=(frames // step,),
        in_specs=[block],
        out_specs=[block, pl.BlockSpec((8, step), lambda i: (0, i))],
        out_shape=[
            jax.ShapeDtypeStruct(coords.shape, jnp.bfloat16),
            jax.ShapeDtypeStruct((8, frames), jnp.float32),
        ],
        compiler_params=pltpu.CompilerParams(dimension_semantics=("arbitrary",), vmem_limit_bytes=8 << 20),
        cost_estimate=pl.CostEstimate(flops=10 * 3 * frames * ATOMS, bytes_accessed=6 << 20, transcendentals=0),
        name="columns",
    )(pltpu.with_memory_space_constraint(coords, pltpu.HBM))


def pair_kernel(mine, other, out):
    for k in range(3):
        for i, ref in enumerate((mine, other)):
            c = centred(ref[k]).astype(jnp.bfloat16).astype(jnp.float32)
            out[k, 32 * i : 32 * i + 32, :] = (c * (4.0 / ATOMS)).astype(jnp.bfloat16)


def line_kernel(p0, p1, p2, p3, out, sent, sem):
    for i, ref in enumerate((p0, p1, p2, p3)):
        out[:, 64 * i : 64 * i + 64, :] = ref[...]
    copy = pltpu.make_async_copy(out, sent, sem)
    copy.start()
    copy.wait()


def line_call(pieces):
    vmem = pl.BlockSpec(memory_space=pltpu.VMEM)
    shape = (3, 256, ATOMS)
    return pl.pallas_call(
        line_kernel,
        out_shape=[jax.ShapeDtypeStruct(shape, jnp.bfloat16), pltpu.HBM(shape, jnp.bfloat16)],
        in_specs=[vmem] * 4,
        out_specs=[vmem, pl.BlockSpec(memory_space=pltpu.HBM)],
        scratch_shapes=[pltpu.SemaphoreType.DMA],
        compiler_params=pltpu.CompilerParams(vmem_limit_bytes=8 << 20),
        name="line",
    )(*pieces)


def newton_slice(p, u):
    def g(i, j):
        return p[0][i] * p[0][j] + p[1][i] * p[1][j] + p[2][i] * p[2][j]

    g00, g11, g22, g01, g02 = g(0, 0), g(1, 1), g(2, 2), g(0, 1), g(0, 2)
    c0 = p[1][1] * p[2][2] - p[2][1] * p[1][2]
    c1 = p[2][1] * p[0][2] - p[0][1] * p[2][2]
    c2 = p[0][1] * p[1][2] - p[1][1] * p[0][2]
    det = p[0][0] * c0 + p[1][0] * c1 + p[2][0] * c2
    pair = g11 + g22
    q = g00 + pair
    minors = (g00 * pair - g01 * g01 - g02 * g02) + (c0 * c0 + c1 * c1 + c2 * c2)
    twice = det + det
    x = u
    for _ in range(NEWTON):
        a = x * x - q
        x = (a * (0.75 * a + q) + minors) / (a * x - twice)
    return u - x


def dist_kernel(ns, *refs):
    rows = refs[:ns]
    cols, cn, sw = refs[ns : ns + 3]
    outs, t_out = refs[ns + 3 : ns + 5], refs[ns + 5]
    bufs, rn, kept, sems = refs[ns + 6 : ns + 8], refs[ns + 8], refs[ns + 9 : ns + 11], refs[ns + 11]
    nb = rn.shape[0]
    per = nb // ns
    ct = pl.program_id(0)
    last = pl.num_programs(0) - 1

    def frames(rb):
        r = (rb % per) * TR
        return rows[rb // per][:, r : r + TR, :]

    def products(rb, at, buf, units):
        c0 = pl.multiple_of(at * TC, TC)
        lhs = frames(rb).reshape(3 * TR, ATOMS)
        for b, n in units:
            buf[b, :, n * 256 : n * 256 + 256] = lax.dot_general(
                lhs, cols[b, pl.ds(c0 + n * 256, 256), :], (((1,), (1,)), ((), ())), preferred_element_type=jnp.float32
            )

    def newton(rb, buf, slices):
        for r, c in slices:
            p = [[buf[b, a * TR + r : a * TR + r + 16, c : c + 128] for b in range(3)] for a in range(3)]
            u = rn[rb, r : r + 16] + cn[0:1, c : c + 128]
            d = newton_slice(p, u)
            h = d.astype(jnp.bfloat16)
            kept[0][ct, rb * TR + r : rb * TR + r + 16, c : c + 128] = h
            kept[1][ct, rb * TR + r : rb * TR + r + 16, c : c + 128] = (d - h.astype(jnp.float32)).astype(jnp.bfloat16)

    def stores(at, rb):
        rows_at = pl.ds(rb * TR, TR)
        return [
            pltpu.make_async_copy(
                kept[i].at[at, rows_at, :], outs[i].at[rows_at, pl.ds(pl.multiple_of(at * TC, TC), TC)], sems.at[i, at, rb]
            )
            for i in range(2)
        ]

    def panel(rb):
        at = slice(rb * TR, rb * TR + TR)
        w = sw[:, pl.ds(pl.multiple_of(ct * TC, TC), TC)]
        dims = (((1,), (1,)), ((), ()))
        t_out[at, :] += lax.dot_general(
            kept[0][ct, at, :], w, dims, preferred_element_type=jnp.float32
        ) + lax.dot_general(kept[1][ct, at, :], w, dims, preferred_element_type=jnp.float32)

    units = [(b, n) for n in range(TC // 256) for b in range(3)]
    slices = [(r, c) for r in range(0, TR, 16) for c in range(0, TC, 128)]
    share = -(-len(slices) // len(units))

    @pl.when(ct == 0)
    def _():
        t_out[...] = jnp.zeros_like(t_out)
        for rb in range(nb):
            w = frames(rb).astype(jnp.float32)
            n = jnp.sum(jnp.sum(w * w, axis=0), axis=1, keepdims=True) * (2.0 * ATOMS / 16.0)
            rn[rb] = jnp.broadcast_to(n, (TR, 128))
        products(0, 0, bufs[0], units)

    for rb in range(nb):
        after, at = (rb + 1, ct) if rb + 1 < nb else (0, jnp.minimum(ct + 1, last))

        @pl.when(ct <= last)
        def _(rb=rb, after=after, at=at):
            for i in range(len(units)):
                newton(rb, bufs[rb % 2], slices[i * share : (i + 1) * share])
                products(after, at, bufs[(rb + 1) % 2], units[i : i + 1])
                if i == 2 and rb > 0:
                    panel(rb - 1)

        for copy in stores(ct, rb):
            copy.start()

    panel(nb - 1)

    @pl.when(ct == last)
    def _():
        for at in range(sems.shape[1]):
            for rb in range(nb):
                for copy in stores(at, rb):
                    copy.wait()


def whole(a):
    return pl.BlockSpec(a.shape, lambda *_: (0,) * a.ndim)


def dist_call(sources, cols, cn, sw):
    nc = cols.shape[1]
    r = sum(a.shape[1] for a in sources)
    return pl.pallas_call(
        functools.partial(dist_kernel, len(sources)),
        grid=(nc // TC,),
        in_specs=[whole(a) for a in sources]
        + [whole(cols), pl.BlockSpec((8, TC), lambda c: (0, c)), whole(sw)],
        out_specs=[
            pl.BlockSpec(memory_space=pltpu.HBM),
            pl.BlockSpec(memory_space=pltpu.HBM),
            pl.BlockSpec((r, 256), lambda c: (0, 0)),
        ],
        out_shape=[
            pltpu.HBM((r, nc), jnp.bfloat16),
            pltpu.HBM((r, nc), jnp.bfloat16),
            jax.ShapeDtypeStruct((r, 256), jnp.float32),
        ],
        scratch_shapes=[
            pltpu.VMEM((3, 3 * TR, TC), jnp.float32),
            pltpu.VMEM((3, 3 * TR, TC), jnp.float32),
            pltpu.VMEM((r // TR, TR, 128), jnp.float32),
            pltpu.VMEM((nc // TC, r, TC), jnp.bfloat16),
            pltpu.VMEM((nc // TC, r, TC), jnp.bfloat16),
            pltpu.SemaphoreType.DMA((2, nc // TC, r // TR)),
        ],
        compiler_params=pltpu.CompilerParams(dimension_semantics=("arbitrary",), vmem_limit_bytes=20 << 20),
        cost_estimate=pl.CostEstimate(
            flops=r * nc * 9 * 2 * ATOMS, bytes_accessed=8 << 20, transcendentals=r * nc * NEWTON
        ),
    )(*sources, cols, cn, sw)


PIECES = [(dy, i, o) for dy in range(2) for i in range(4) for o in range(4)]
CHUNK_START = (0, 256, 768)


def place(dy, i, o):
    return (o + 1) // 2, (o == 2) * 256 + (i * 2 + dy) * 32


def owner_of(dy, i, o):
    me, core = lax.axis_index("col"), lax.axis_index("row") % 2
    y, x, z = me // 16, (me // 4) % 4, me % 4
    dx = OFFSETS[o] + core * (OFFSETS[i] - OFFSETS[o])
    dz = OFFSETS[i] + core * (OFFSETS[o] - OFFSETS[i])
    return ((y + dy) % 2) * 16 + ((x + dx + 4) % 4) * 4 + (z + dz + 4) % 4


def lanes(shape):
    return lax.broadcasted_iota(jnp.int32, shape, len(shape) - 1)


def pack_kernel(t0, t1, t2, bm, out):
    ts = (t0, t1, t2)
    lane16, lane8 = lanes((16, 128)), lanes((8, 128))
    means = jnp.broadcast_to(bm[...], (8, 128))
    for piece in PIECES:
        dest = owner_of(*piece)
        chunk, at = place(*piece)
        full, sums = [], []
        for r in (at, at + 16):
            t = ts[chunk][r : r + 16, 0:128]
            full.append(t + pltpu.roll(t, 64, 1))
            sums.append(ts[chunk][r : r + 16, 128:256])
        out[dest, 0:16, :] = jnp.where(lane16 < 64, full[0], full[1])
        ext = jnp.where(lane8 < 16, sums[0][0:8], sums[0][8:16])
        ext = jnp.where(lane8 < 32, ext, sums[1][0:8])
        ext = jnp.where(lane8 < 48, ext, sums[1][8:16])
        out[dest, 16:24, :] = jnp.where(lane8 < 64, ext, means)


def owner_kernel(got, out):
    lane = lanes((8, 128))

    def spread(ext):
        one = lambda k: jnp.broadcast_to(ext[:, k : k + 1], (8, 128))
        return jnp.where(lane < 64, one(0), one(32)), jnp.where(lane < 64, one(16), one(48))

    zero = jnp.zeros((8, 128), jnp.float32)
    a, b, e = zero, zero, zero
    for src in range(got.shape[0]):
        ext = got[src, 16:24, :]
        bm = jnp.where(lane < 64, pltpu.roll(ext, 64, 1), ext)
        r0, r1 = spread(ext)
        a = a + (got[src, 0:8, :] + r0 * bm)
        b = b + (got[src, 8:16, :] + r1 * bm)
        e = e + ext
    bm = jnp.where(lane < 64, pltpu.roll(e, 64, 1), e) * (1.0 / got.shape[0])
    r0, r1 = spread(e)
    a = a - r0 * bm
    b = b - r1 * bm
    sub = lax.broadcasted_iota(jnp.int32, (8, 128), 0)
    y = jnp.sum(r0 * a + r1 * b, axis=0, keepdims=True)
    tot = jnp.sum(r0 + r1, axis=0, keepdims=True)
    ext = jnp.where(sub == 0, jnp.broadcast_to(y, (8, 128)), jnp.broadcast_to(tot, (8, 128)))
    for dst in range(got.shape[0]):
        out[dst, 0:8, :] = a
        out[dst, 8:16, :] = b
        out[dst, 16:24, :] = ext


def panel_kernel(got, left, tc_out, stat, arr):
    n = got.shape[0]
    lane1 = lanes((1, 128))

    def both(v):
        return v + pltpu.roll(v, 64, 1)

    total = jnp.sum(jnp.sum(got[:, 0:16, :], axis=0), axis=0, keepdims=True)
    mean = both(total) * (1.0 / (32 * n))
    ext = jnp.sum(got[:, 16:24, :], axis=0)
    y, rows = both(ext[0:1]), both(ext[1:2])
    x = got[:, 0:16, :] - mean
    flat = x.reshape(n * 16, 128)
    g = lax.dot_general(flat, flat, (((0,), (0,)), ((), ())), precision=HIGHEST, preferred_element_type=jnp.float32)
    stat[0:64, :] = g[0:64, :] + pltpu.roll(g[64:128, :], 64, 1)
    sub = lax.broadcasted_iota(jnp.int32, (8, 128), 0)
    tile = jnp.where(sub == 0, mean, jnp.where(sub == 1, y, rows))
    stat[64:72, :] = jnp.broadcast_to(tile, (8, 128))
    for b in range(n):
        tc_out[b * 32 : b * 32 + 16, :] = x[b, :, 0:64]
        tc_out[b * 32 + 16 : b * 32 + 32, :] = x[b, :, 64:128]
    for piece in PIECES:
        src = owner_of(*piece)
        t = got[src, 0:16, :] - mean
        chunk, r = place(*piece)
        r += CHUNK_START[chunk]
        arr[r : r + 16, :] = t
        arr[r + 16 : r + 32, :] = pltpu.roll(t, 64, 1)
    pt = jnp.transpose(arr[...])[0:64, :]
    h = pt.astype(jnp.bfloat16)
    left[0:64, :] = h
    left[64:128, :] = (pt - h.astype(jnp.float32)).astype(jnp.bfloat16)
    left[128:144, :] = jnp.ones((16, pt.shape[1]), jnp.bfloat16)


def image_kernel(me, left, h0, l0, h1, l1, h2, l2, *refs):
    outs, late, sems = refs[:4], refs[4], refs[5]
    k = pl.program_id(0)
    copies = [pltpu.make_async_copy(ref, late.at[i], sems.at[i]) for i, ref in enumerate((h2, l2))]

    @pl.when(k == 0)
    def _():
        for copy in copies:
            copy.start()

    acc = jnp.zeros((144, NC), jnp.float32)
    for at, refs in zip(CHUNK_START, ((h0, l0), (h1, l1))):
        for ref in refs:
            acc += jnp.dot(left[:, at : at + ref.shape[0]], ref[...], preferred_element_type=jnp.float32)

    @pl.when(k == 0)
    def _():
        for copy in copies:
            copy.wait()

    mine = pl.ds(pl.multiple_of((me[0] ^ k) * NC, NC), NC)
    for i in range(2):
        acc += jnp.dot(left[:, CHUNK_START[2] :], late[i, :, mine], preferred_element_type=jnp.float32)
    for j in range(4):

        @pl.when(k == j)
        def _(j=j):
            outs[j][0:64, :] = acc[0:64] + acc[64:128]
            outs[j][64:72, :] = acc[128:136]


def image_call(me, left, chunks):
    flat = [a for c in chunks for a in c[:2]]
    flat[4:] = [pltpu.with_memory_space_constraint(a, pltpu.HBM) for a in flat[4:]]
    spec = lambda a: pl.BlockSpec((a.shape[0], NC), lambda k, me: (0, me[0] ^ k))
    hbm = pl.BlockSpec(memory_space=pltpu.HBM)
    return pl.pallas_call(
        image_kernel,
        grid_spec=pltpu.PrefetchScalarGridSpec(
            num_scalar_prefetch=1,
            grid=(4,),
            in_specs=[pl.BlockSpec(left.shape, lambda k, me: (0, 0))] + [spec(a) for a in flat[:4]] + [hbm] * 2,
            out_specs=[pl.BlockSpec((72, NC), lambda k, me: (0, 0))] * 4,
            scratch_shapes=[pltpu.VMEM((2, *flat[4].shape), jnp.bfloat16), pltpu.SemaphoreType.DMA((2,))],
        ),
        out_shape=[jax.ShapeDtypeStruct((72, NC), jnp.float32)] * 4,
        compiler_params=pltpu.CompilerParams(dimension_semantics=("arbitrary",), vmem_limit_bytes=16 << 20),
        cost_estimate=pl.CostEstimate(flops=2 * 2 * 256 * 1024 * 1024, bytes_accessed=5 << 20, transcendentals=0),
        name="image",
    )(me, left, *flat)


def factor_kernel(s0, s1, s2, s3, m_out, d_out):
    stats = (s0, s1, s2, s3)

    def total(lo, hi):
        return (s0[lo:hi, :] + s1[lo:hi, :]) + (s2[lo:hi, :] + s3[lo:hi, :])

    mean = total(64, 65) * 0.25
    offs = [s[64:65, :] - mean for s in stats]
    y = total(65, 66) - mean * total(66, 67)
    sub = lax.broadcasted_iota(jnp.int32, (8, 128), 0)
    deltas = jnp.zeros((8, 128), jnp.float32)
    for k in range(4):
        deltas = jnp.where(sub == k, offs[k], deltas)
    d_out[...] = jnp.where(sub == 4, y * (1.0 / CF), deltas)
    outer = lax.dot_general(
        deltas, deltas, (((0,), (0,)), ((), ())), precision=HIGHEST, preferred_element_type=jnp.float32
    )
    gram = (total(0, 64) + outer[0:64, :] * (RF // 4)) * (1.0 / (16 * RF))
    lane = lanes((64, 128))
    row = lax.broadcasted_iota(jnp.int32, (64, 128), 0)
    a = jnp.where(lane < 64, gram, jnp.where(lane - 64 == row, 1.0, 0.0))
    tiles = [a[8 * t : 8 * t + 8, :] for t in range(8)]
    eighth = lax.broadcasted_iota(jnp.int32, (8, 128), 0)
    for t in range(8):
        cols = [[jnp.broadcast_to(tiles[i][:, 8 * t + j : 8 * t + j + 1], (8, 128)) for i in range(t, 8)] for j in range(8)]
        rest = tiles[t:]
        for j in range(8):
            spread = lambda v: jnp.broadcast_to(v[j : j + 1, :], (8, 128))
            pivot = spread(cols[j][0])
            inv = 1.0 / pivot
            row_j = spread(rest[0])
            m_out[8 * t + j : 8 * t + j + 1, :] = (row_j * (lax.rsqrt(pivot) * -0.25))[0:1, :]
            below = [v * inv for v in cols[j]]
            below[0] = jnp.where(eighth > j, below[0], 0.0)
            for l in range(j + 1, 8):
                top = spread(cols[l][0])
                cols[l] = [v - m * top for v, m in zip(cols[l], below)]
            rest = [v - m * row_j for v, m in zip(rest, below)]
        tiles[t:] = rest


def join_kernel(w, g1, g2, g3, m, d, out):
    parts = (w[0:64] + g1[0:64]) + (g2[0:64] + g3[0:64])
    sub = lax.broadcasted_iota(jnp.int32, (8, NC), 0)
    sums = jnp.where(sub == 4, -1.0, 0.0)
    for k, ref in enumerate((w, g1, g2, g3)):
        sums = jnp.where(sub == k, ref[64:72], sums)
    add = lax.dot_general(
        d[...], sums, (((0,), (0,)), ((), ())), precision=HIGHEST, preferred_element_type=jnp.float32
    )
    inv = pltpu.roll(m[...], 64, 1)[:, 0:64]
    res = jnp.dot(inv, parts + add[0:64], precision=HIGHEST, preferred_element_type=jnp.float32)
    out[...] = (res * (-0.25 / RF**0.5)).astype(jnp.bfloat16)


def basis_kernel(tc, m, d, out):
    inv = pltpu.roll(m[...], 64, 1)[:, 0:64]
    x = tc[...] + d[0:1, 0:64]
    out[...] = lax.dot_general(
        inv, x, (((1,), (1,)), ((), ())), precision=HIGHEST, preferred_element_type=jnp.float32
    )


def spread_kernel(i0, i1, i2, i3, out):
    me = lax.axis_index("row")
    for k, ref in enumerate((i0, i1, i2, i3)):
        at = pl.multiple_of((me ^ k) * NC, NC)
        out[:, pl.ds(at, NC)] = ref[...].astype(jnp.float32)


def call(kernel, outs, *args, scratch=(), **kw):
    return pl.pallas_call(
        kernel,
        out_shape=outs,
        in_specs=[pl.BlockSpec(memory_space=pltpu.VMEM)] * len(args),
        out_specs=jax.tree.map(lambda _: pl.BlockSpec(memory_space=pltpu.VMEM), outs),
        scratch_shapes=scratch,
        compiler_params=pltpu.CompilerParams(vmem_limit_bytes=8 << 20),
        **kw,
    )(*args)


def index(core, lo, y, x, z):
    return (lo * 2 + core) * 32 + ((y % 2) * 4 + x % 4) * 4 + z % 4


DEVICES = [(c, w, y, x, z) for c in range(2) for w in range(2) for y in range(2) for x in range(4) for z in range(4)]


def shift(a, dy=0, inner=0, outer=0):
    pairs = []
    for c, w, y, x, z in DEVICES:
        dx, dz = (inner, outer) if c else (outer, inner)
        pairs.append((index(c, w, y, x, z), index(c, w, y + dy, x + dx, z + dz)))
    return lax.ppermute(a, ("row", "col"), pairs)


def swap(a, k):
    return lax.ppermute(a, "row", [(r, r ^ k) for r in range(4)])


def from_three(a, axis):
    return [shift(a, **{axis: -o}) for o in OFFSETS[1:]]


def body(row_coords, col_coords, start_block):
    f32 = jnp.float32
    other = shift(row_coords, dy=1)
    cols, cn = column_call(col_coords)
    pair = call(pair_kernel, jax.ShapeDtypeStruct((3, 64, ATOMS), jnp.bfloat16), row_coords, other)
    line, sent = line_call([pair, *from_three(pair, "inner")])
    far = []
    for o in OFFSETS[1:]:
        far.append(shift(sent, outer=-o))

    start = start_block.T
    block_mean = jnp.mean(start, axis=1)
    start = start - block_mean[:, None]
    start_hi = lax.reduce_precision(start, 8, 7)
    ones = jnp.ones((128, start.shape[1]), jnp.bfloat16)
    sw = jnp.concatenate([start_hi.astype(jnp.bfloat16), (start - start_hi).astype(jnp.bfloat16), ones], axis=0)
    bm = jnp.concatenate([block_mean, block_mean])[None, :]

    chunks = []
    for rows in ([line], far[:2], far[2:]):
        chunks.append(dist_call(rows, cols, cn, sw))
    n = lax.axis_size("col")
    packed = jax.ShapeDtypeStruct((n, 24, 128), f32)
    sent = call(pack_kernel, packed, *(c[2] for c in chunks), bm)
    got = lax.all_to_all(sent, "col", 0, 0, tiled=True)
    totals = call(owner_kernel, packed, got)
    got = lax.all_to_all(totals, "col", 0, 0, tiled=True)
    left, tc, stat = call(
        panel_kernel,
        (
            jax.ShapeDtypeStruct((144, 32 * n), jnp.bfloat16),
            jax.ShapeDtypeStruct((32 * n, K), f32),
            jax.ShapeDtypeStruct((72, 128), f32),
        ),
        got,
        scratch=[pltpu.VMEM((32 * n, 128), f32)],
    )
    me = lax.axis_index("row").reshape(1)
    stats = [stat]
    for k in (1, 2, 3):
        stats.append(swap(stat, k))
    partial = image_call(me, left, chunks)
    arrived = [partial[0], *(swap(partial[k], k) for k in (1, 2, 3))]
    m, d = call(
        factor_kernel, (jax.ShapeDtypeStruct((64, 128), f32), jax.ShapeDtypeStruct((8, 128), f32)), *stats
    )
    part = call(join_kernel, jax.ShapeDtypeStruct((64, NC), jnp.bfloat16), *arrived, m, d)
    parts = [part, *(swap(part, k) for k in (1, 2, 3))]
    basis = call(basis_kernel, jax.ShapeDtypeStruct((K, 32 * n), f32), tc, m, d)
    image = call(spread_kernel, jax.ShapeDtypeStruct((K, 4 * NC), f32), *parts)
    return (basis.T, image.T)


def solution(mesh):
    in_specs = (P(None, ("row", "col"), None), P(None, "col", None), P("col", None))
    out_specs = (P("row", None), P("col", None))
    return jax.shard_map(body, mesh=mesh, in_specs=in_specs, out_specs=out_specs, check_vma=False)
```

```python
import functools

import jax
import jax.numpy as jnp
from jax import lax
from jax.experimental import pallas as pl
from jax.experimental.pallas import tpu as pltpu
from jax.sharding import PartitionSpec as P


ATOMS = 512
NEWTON = 8
K = 64
TR = 128
TC = 512
SR, SC = 16, 512
UNIT_AT = (0, 1, 2, 3, 4, 5)
PANEL_AT = 6
NC = 256
RF = 4096
CF = 32768
HIGHEST = lax.Precision.HIGHEST
OFFSETS = (0, -1, 1, 2)


def centred(coords):
    wide = coords.astype(jnp.float32)
    return wide - jnp.sum(wide, axis=-1, keepdims=True) * (1.0 / ATOMS)


def column_kernel(coords, out, norm):
    total = None
    for k in range(3):
        c = centred(coords[k]).astype(jnp.bfloat16)
        out[k] = c
        w = c.astype(jnp.float32)
        part = jnp.sum(w * w, axis=1, keepdims=True)
        total = part if total is None else total + part
    spread = jnp.broadcast_to(total * (2.0 / ATOMS), (total.shape[0], 128))
    norm[...] = jnp.transpose(spread)[0:8, :]


def column_call(coords):
    frames, step = coords.shape[1], 256
    block = pl.BlockSpec((3, step, ATOMS), lambda i: (0, i, 0))
    return pl.pallas_call(
        column_kernel,
        grid=(frames // step,),
        in_specs=[block],
        out_specs=[block, pl.BlockSpec((8, step), lambda i: (0, i))],
        out_shape=[
            jax.ShapeDtypeStruct(coords.shape, jnp.bfloat16),
            jax.ShapeDtypeStruct((8, frames), jnp.float32),
        ],
        compiler_params=pltpu.CompilerParams(dimension_semantics=("arbitrary",), vmem_limit_bytes=8 << 20),
        cost_estimate=pl.CostEstimate(flops=10 * 3 * frames * ATOMS, bytes_accessed=6 << 20, transcendentals=0),
        name="columns",
    )(pltpu.with_memory_space_constraint(coords, pltpu.HBM))


def pair_kernel(mine, other, out):
    for k in range(3):
        for i, ref in enumerate((mine, other)):
            c = centred(ref[k]).astype(jnp.bfloat16).astype(jnp.float32)
            out[k, 32 * i : 32 * i + 32, :] = (c * (4.0 / ATOMS)).astype(jnp.bfloat16)


def line_kernel(p0, p1, p2, p3, out, sent, sem):
    for i, ref in enumerate((p0, p1, p2, p3)):
        out[:, 64 * i : 64 * i + 64, :] = ref[...]
    copy = pltpu.make_async_copy(out, sent, sem)
    copy.start()
    copy.wait()


def line_call(pieces):
    vmem = pl.BlockSpec(memory_space=pltpu.VMEM)
    shape = (3, 256, ATOMS)
    return pl.pallas_call(
        line_kernel,
        out_shape=[jax.ShapeDtypeStruct(shape, jnp.bfloat16), pltpu.HBM(shape, jnp.bfloat16)],
        in_specs=[vmem] * 4,
        out_specs=[vmem, pl.BlockSpec(memory_space=pltpu.HBM)],
        scratch_shapes=[pltpu.SemaphoreType.DMA],
        compiler_params=pltpu.CompilerParams(vmem_limit_bytes=8 << 20),
        name="line",
    )(*pieces)


def newton_slice(p, u):
    def g(i, j):
        return p[0][i] * p[0][j] + p[1][i] * p[1][j] + p[2][i] * p[2][j]

    g00, g11, g22, g01, g02 = g(0, 0), g(1, 1), g(2, 2), g(0, 1), g(0, 2)
    c0 = p[1][1] * p[2][2] - p[2][1] * p[1][2]
    c1 = p[2][1] * p[0][2] - p[0][1] * p[2][2]
    c2 = p[0][1] * p[1][2] - p[1][1] * p[0][2]
    det = p[0][0] * c0 + p[1][0] * c1 + p[2][0] * c2
    pair = g11 + g22
    q = g00 + pair
    minors = (g00 * pair - g01 * g01 - g02 * g02) + (c0 * c0 + c1 * c1 + c2 * c2)
    twice = det + det
    x = u
    for _ in range(NEWTON):
        a = x * x - q
        x = (a * (0.75 * a + q) + minors) / (a * x - twice)
    return u - x


def dist_kernel(ns, *refs):
    rows = refs[:ns]
    cols, cn, sw = refs[ns : ns + 3]
    outs, t_out = refs[ns + 3 : ns + 5], refs[ns + 5]
    bufs, rn, kept, sems = refs[ns + 6 : ns + 8], refs[ns + 8], refs[ns + 9], refs[ns + 10]
    nb = rn.shape[0]
    per = nb // ns
    ct = pl.program_id(0)
    last = pl.num_programs(0) - 1

    def frames(rb):
        r = (rb % per) * TR
        return rows[rb // per][:, r : r + TR, :]

    def products(rb, at, buf, units):
        c0 = pl.multiple_of(at * TC, TC)
        lhs = frames(rb).reshape(3 * TR, ATOMS)
        for b, n in units:
            buf[b, :, n * 256 : n * 256 + 256] = lax.dot_general(
                lhs, cols[b, pl.ds(c0 + n * 256, 256), :], (((1,), (1,)), ((), ())), preferred_element_type=jnp.float32
            )

    def newton(rb, buf, slices):
        for r, c in slices:
            p = [[buf[b, a * TR + r : a * TR + r + SR, c : c + SC] for b in range(3)] for a in range(3)]
            u = rn[rb, r : r + SR, 0:SC] + cn[0:1, c : c + SC]
            d = newton_slice(p, u)
            h = d.astype(jnp.bfloat16)
            kept[ct, rb, 0, r : r + SR, c : c + SC] = h
            kept[ct, rb, 1, r : r + SR, c : c + SC] = (d - h.astype(jnp.float32)).astype(jnp.bfloat16)

    def stores(at, rb):
        rows_at = pl.ds(rb * TR, TR)
        return [
            pltpu.make_async_copy(
                kept.at[at, rb, i], outs[i].at[rows_at, pl.ds(pl.multiple_of(at * TC, TC), TC)], sems.at[i, at, rb]
            )
            for i in range(2)
        ]

    def panel(rb):
        w = sw[:, pl.ds(pl.multiple_of(ct * TC, TC), TC)]
        both = kept[ct, rb].reshape(2 * TR, TC)
        t = lax.dot_general(both, w, (((1,), (1,)), ((), ())), preferred_element_type=jnp.float32)
        t_out[rb * TR : rb * TR + TR, :] += t[0:TR] + t[TR : 2 * TR]

    units = [(b, n) for n in range(TC // 256) for b in range(3)]
    slices = [(r, c) for r in range(0, TR, SR) for c in range(0, TC, SC)]

    @pl.when(ct == 0)
    def _():
        t_out[...] = jnp.zeros_like(t_out)
        for rb in range(nb):
            w = frames(rb).astype(jnp.float32)
            n = jnp.sum(jnp.sum(w * w, axis=0), axis=1, keepdims=True) * (2.0 * ATOMS / 16.0)
            rn[rb] = jnp.broadcast_to(n, (TR, SC))
        products(0, 0, bufs[0], units)

    for rb in range(nb):
        after, at = (rb + 1, ct) if rb + 1 < nb else (0, jnp.minimum(ct + 1, last))

        @pl.when(ct <= last)
        def _(rb=rb, after=after, at=at):
            for i in range(len(slices)):
                if i in UNIT_AT:
                    j = UNIT_AT.index(i)
                    products(after, at, bufs[(rb + 1) % 2], units[j : j + 1])
                if i == PANEL_AT and rb > 0:
                    panel(rb - 1)
                newton(rb, bufs[rb % 2], slices[i : i + 1])

        for copy in stores(ct, rb):
            copy.start()

    panel(nb - 1)

    @pl.when(ct == last)
    def _():
        for at in range(sems.shape[1]):
            for rb in range(nb):
                for copy in stores(at, rb):
                    copy.wait()


def whole(a):
    return pl.BlockSpec(a.shape, lambda *_: (0,) * a.ndim)


def dist_call(sources, cols, cn, sw):
    nc = cols.shape[1]
    r = sum(a.shape[1] for a in sources)
    return pl.pallas_call(
        functools.partial(dist_kernel, len(sources)),
        grid=(nc // TC,),
        in_specs=[whole(a) for a in sources]
        + [whole(cols), pl.BlockSpec((8, TC), lambda c: (0, c)), whole(sw)],
        out_specs=[
            pl.BlockSpec(memory_space=pltpu.HBM),
            pl.BlockSpec(memory_space=pltpu.HBM),
            pl.BlockSpec((r, 256), lambda c: (0, 0)),
        ],
        out_shape=[
            pltpu.HBM((r, nc), jnp.bfloat16),
            pltpu.HBM((r, nc), jnp.bfloat16),
            jax.ShapeDtypeStruct((r, 256), jnp.float32),
        ],
        scratch_shapes=[
            pltpu.VMEM((3, 3 * TR, TC), jnp.float32),
            pltpu.VMEM((3, 3 * TR, TC), jnp.float32),
            pltpu.VMEM((r // TR, TR, SC), jnp.float32),
            pltpu.VMEM((nc // TC, r // TR, 2, TR, TC), jnp.bfloat16),
            pltpu.SemaphoreType.DMA((2, nc // TC, r // TR)),
        ],
        compiler_params=pltpu.CompilerParams(dimension_semantics=("arbitrary",), vmem_limit_bytes=20 << 20),
        cost_estimate=pl.CostEstimate(
            flops=r * nc * 9 * 2 * ATOMS, bytes_accessed=8 << 20, transcendentals=r * nc * NEWTON
        ),
    )(*sources, cols, cn, sw)


PIECES = [(dy, i, o) for dy in range(2) for i in range(4) for o in range(4)]
CHUNK_START = (0, 256, 768)


def place(dy, i, o):
    return (o + 1) // 2, (o == 2) * 256 + (i * 2 + dy) * 32


def owner_of(dy, i, o):
    me, core = lax.axis_index("col"), lax.axis_index("row") % 2
    y, x, z = me // 16, (me // 4) % 4, me % 4
    dx = OFFSETS[o] + core * (OFFSETS[i] - OFFSETS[o])
    dz = OFFSETS[i] + core * (OFFSETS[o] - OFFSETS[i])
    return ((y + dy) % 2) * 16 + ((x + dx + 4) % 4) * 4 + (z + dz + 4) % 4


def lanes(shape):
    return lax.broadcasted_iota(jnp.int32, shape, len(shape) - 1)


def pack_kernel(t0, t1, t2, bm, out):
    ts = (t0, t1, t2)
    lane16, lane8 = lanes((16, 128)), lanes((8, 128))
    means = jnp.broadcast_to(bm[...], (8, 128))
    for piece in PIECES:
        dest = owner_of(*piece)
        chunk, at = place(*piece)
        full, sums = [], []
        for r in (at, at + 16):
            t = ts[chunk][r : r + 16, 0:128]
            full.append(t + pltpu.roll(t, 64, 1))
            sums.append(ts[chunk][r : r + 16, 128:256])
        out[dest, 0:16, :] = jnp.where(lane16 < 64, full[0], full[1])
        ext = jnp.where(lane8 < 16, sums[0][0:8], sums[0][8:16])
        ext = jnp.where(lane8 < 32, ext, sums[1][0:8])
        ext = jnp.where(lane8 < 48, ext, sums[1][8:16])
        out[dest, 16:24, :] = jnp.where(lane8 < 64, ext, means)


def owner_kernel(got, out):
    lane = lanes((8, 128))

    def spread(ext):
        one = lambda k: jnp.broadcast_to(ext[:, k : k + 1], (8, 128))
        return jnp.where(lane < 64, one(0), one(32)), jnp.where(lane < 64, one(16), one(48))

    zero = jnp.zeros((8, 128), jnp.float32)
    a, b, e = zero, zero, zero
    for src in range(got.shape[0]):
        ext = got[src, 16:24, :]
        bm = jnp.where(lane < 64, pltpu.roll(ext, 64, 1), ext)
        r0, r1 = spread(ext)
        a = a + (got[src, 0:8, :] + r0 * bm)
        b = b + (got[src, 8:16, :] + r1 * bm)
        e = e + ext
    bm = jnp.where(lane < 64, pltpu.roll(e, 64, 1), e) * (1.0 / got.shape[0])
    r0, r1 = spread(e)
    a = a - r0 * bm
    b = b - r1 * bm
    sub = lax.broadcasted_iota(jnp.int32, (8, 128), 0)
    y = jnp.sum(r0 * a + r1 * b, axis=0, keepdims=True)
    tot = jnp.sum(r0 + r1, axis=0, keepdims=True)
    ext = jnp.where(sub == 0, jnp.broadcast_to(y, (8, 128)), jnp.broadcast_to(tot, (8, 128)))
    for dst in range(got.shape[0]):
        out[dst, 0:8, :] = a
        out[dst, 8:16, :] = b
        out[dst, 16:24, :] = ext


def panel_kernel(got, left, tc_out, stat, arr):
    n = got.shape[0]
    lane1 = lanes((1, 128))

    def both(v):
        return v + pltpu.roll(v, 64, 1)

    total = jnp.sum(jnp.sum(got[:, 0:16, :], axis=0), axis=0, keepdims=True)
    mean = both(total) * (1.0 / (32 * n))
    ext = jnp.sum(got[:, 16:24, :], axis=0)
    y, rows = both(ext[0:1]), both(ext[1:2])
    x = got[:, 0:16, :] - mean
    flat = x.reshape(n * 16, 128)
    g = lax.dot_general(flat, flat, (((0,), (0,)), ((), ())), precision=HIGHEST, preferred_element_type=jnp.float32)
    stat[0:64, :] = g[0:64, :] + pltpu.roll(g[64:128, :], 64, 1)
    sub = lax.broadcasted_iota(jnp.int32, (8, 128), 0)
    tile = jnp.where(sub == 0, mean, jnp.where(sub == 1, y, rows))
    stat[64:72, :] = jnp.broadcast_to(tile, (8, 128))
    for b in range(n):
        tc_out[b * 32 : b * 32 + 16, :] = x[b, :, 0:64]
        tc_out[b * 32 + 16 : b * 32 + 32, :] = x[b, :, 64:128]
    for piece in PIECES:
        src = owner_of(*piece)
        t = got[src, 0:16, :] - mean
        chunk, r = place(*piece)
        r += CHUNK_START[chunk]
        arr[r : r + 16, :] = t
        arr[r + 16 : r + 32, :] = pltpu.roll(t, 64, 1)
    pt = jnp.transpose(arr[...])[0:64, :]
    h = pt.astype(jnp.bfloat16)
    left[0:64, :] = h
    left[64:128, :] = (pt - h.astype(jnp.float32)).astype(jnp.bfloat16)
    left[128:144, :] = jnp.ones((16, pt.shape[1]), jnp.bfloat16)


def image_kernel(left, h0, l0, h1, l1, h2, l2, o0, o1, o2, o3, late, acc, sems):
    copies = [pltpu.make_async_copy(ref, late.at[i], sems.at[i]) for i, ref in enumerate((h2, l2))]
    for copy in copies:
        copy.start()

    def block(k):
        return pl.ds(pl.multiple_of((lax.axis_index("row") ^ k) * NC, NC), NC)

    for k in range(4):
        total = jnp.zeros((144, NC), jnp.float32)
        for at, refs in zip(CHUNK_START, ((h0, l0), (h1, l1))):
            for ref in refs:
                total += jnp.dot(
                    left[:, at : at + ref.shape[0]], ref[:, block(k)], preferred_element_type=jnp.float32
                )
        acc[k] = total
    for copy in copies:
        copy.wait()
    for k, out in enumerate((o0, o1, o2, o3)):
        total = acc[k]
        for i in range(2):
            total += jnp.dot(left[:, CHUNK_START[2] :], late[i, :, block(k)], preferred_element_type=jnp.float32)
        out[0:64, :] = total[0:64] + total[64:128]
        out[64:72, :] = total[128:136]


def image_call(left, chunks):
    flat = [a for c in chunks for a in c[:2]]
    flat[4:] = [pltpu.with_memory_space_constraint(a, pltpu.HBM) for a in flat[4:]]
    vmem = pl.BlockSpec(memory_space=pltpu.VMEM)
    return pl.pallas_call(
        image_kernel,
        in_specs=[vmem] * 5 + [pl.BlockSpec(memory_space=pltpu.HBM)] * 2,
        out_specs=[vmem] * 4,
        scratch_shapes=[
            pltpu.VMEM((2, *flat[4].shape), jnp.bfloat16),
            pltpu.VMEM((4, 144, NC), jnp.float32),
            pltpu.SemaphoreType.DMA((2,)),
        ],
        out_shape=[jax.ShapeDtypeStruct((72, NC), jnp.float32)] * 4,
        compiler_params=pltpu.CompilerParams(vmem_limit_bytes=12 << 20),
        cost_estimate=pl.CostEstimate(flops=2 * 2 * 256 * 1024 * 1024, bytes_accessed=5 << 20, transcendentals=0),
        name="image",
    )(left, *flat)


def factor_kernel(s0, s1, s2, s3, m_out, d_out):
    stats = (s0, s1, s2, s3)

    def total(lo, hi):
        return (s0[lo:hi, :] + s1[lo:hi, :]) + (s2[lo:hi, :] + s3[lo:hi, :])

    mean = total(64, 65) * 0.25
    offs = [s[64:65, :] - mean for s in stats]
    y = total(65, 66) - mean * total(66, 67)
    sub = lax.broadcasted_iota(jnp.int32, (8, 128), 0)
    deltas = jnp.zeros((8, 128), jnp.float32)
    for k in range(4):
        deltas = jnp.where(sub == k, offs[k], deltas)
    d_out[...] = jnp.where(sub == 4, y * (1.0 / CF), deltas)
    outer = lax.dot_general(
        deltas, deltas, (((0,), (0,)), ((), ())), precision=HIGHEST, preferred_element_type=jnp.float32
    )
    gram = (total(0, 64) + outer[0:64, :] * (RF // 4)) * (1.0 / (16 * RF))
    lane = lanes((64, 128))
    row = lax.broadcasted_iota(jnp.int32, (64, 128), 0)
    a = jnp.where(lane < 64, gram, jnp.where(lane - 64 == row, 1.0, 0.0))
    tiles = [a[8 * t : 8 * t + 8, :] for t in range(8)]
    eighth = lax.broadcasted_iota(jnp.int32, (8, 128), 0)
    for t in range(8):
        cols = [[jnp.broadcast_to(tiles[i][:, 8 * t + j : 8 * t + j + 1], (8, 128)) for i in range(t, 8)] for j in range(8)]
        rest = tiles[t:]
        for j in range(8):
            spread = lambda v: jnp.broadcast_to(v[j : j + 1, :], (8, 128))
            pivot = spread(cols[j][0])
            inv = 1.0 / pivot
            row_j = spread(rest[0])
            m_out[8 * t + j : 8 * t + j + 1, :] = (row_j * (lax.rsqrt(pivot) * -0.25))[0:1, :]
            below = [v * inv for v in cols[j]]
            below[0] = jnp.where(eighth > j, below[0], 0.0)
            for l in range(j + 1, 8):
                top = spread(cols[l][0])
                cols[l] = [v - m * top for v, m in zip(cols[l], below)]
            rest = [v - m * row_j for v, m in zip(rest, below)]
        tiles[t:] = rest


def join_kernel(w, g1, g2, g3, m, d, out):
    parts = (w[0:64] + g1[0:64]) + (g2[0:64] + g3[0:64])
    sub = lax.broadcasted_iota(jnp.int32, (8, NC), 0)
    sums = jnp.where(sub == 4, -1.0, 0.0)
    for k, ref in enumerate((w, g1, g2, g3)):
        sums = jnp.where(sub == k, ref[64:72], sums)
    add = lax.dot_general(
        d[...], sums, (((0,), (0,)), ((), ())), precision=HIGHEST, preferred_element_type=jnp.float32
    )
    inv = pltpu.roll(m[...], 64, 1)[:, 0:64]
    res = jnp.dot(inv, parts + add[0:64], precision=HIGHEST, preferred_element_type=jnp.float32)
    out[...] = (res * (-0.25 / RF**0.5)).astype(jnp.bfloat16)


def basis_kernel(tc, m, d, out):
    inv = pltpu.roll(m[...], 64, 1)[:, 0:64]
    x = tc[...] + d[0:1, 0:64]
    out[...] = lax.dot_general(
        inv, x, (((1,), (1,)), ((), ())), precision=HIGHEST, preferred_element_type=jnp.float32
    )


def spread_kernel(i0, i1, i2, i3, out):
    me = lax.axis_index("row")
    for k, ref in enumerate((i0, i1, i2, i3)):
        at = pl.multiple_of((me ^ k) * NC, NC)
        out[:, pl.ds(at, NC)] = ref[...].astype(jnp.float32)


def call(kernel, outs, *args, scratch=(), **kw):
    return pl.pallas_call(
        kernel,
        out_shape=outs,
        in_specs=[pl.BlockSpec(memory_space=pltpu.VMEM)] * len(args),
        out_specs=jax.tree.map(lambda _: pl.BlockSpec(memory_space=pltpu.VMEM), outs),
        scratch_shapes=scratch,
        compiler_params=pltpu.CompilerParams(vmem_limit_bytes=8 << 20),
        **kw,
    )(*args)


def index(core, lo, y, x, z):
    return (lo * 2 + core) * 32 + ((y % 2) * 4 + x % 4) * 4 + z % 4


DEVICES = [(c, w, y, x, z) for c in range(2) for w in range(2) for y in range(2) for x in range(4) for z in range(4)]


def shift(a, dy=0, inner=0, outer=0):
    pairs = []
    for c, w, y, x, z in DEVICES:
        dx, dz = (inner, outer) if c else (outer, inner)
        pairs.append((index(c, w, y, x, z), index(c, w, y + dy, x + dx, z + dz)))
    return lax.ppermute(a, ("row", "col"), pairs)


def swap(a, k):
    return lax.ppermute(a, "row", [(r, r ^ k) for r in range(4)])


def exchanged(arrays):
    got = {k: swap(arrays[k], k) for k in (3, 2, 1)}
    return [got[k] for k in (1, 2, 3)]


def from_three(a, axis):
    return [shift(a, **{axis: -o}) for o in OFFSETS[1:]]


def body(row_coords, col_coords, start_block):
    f32 = jnp.float32
    other = shift(row_coords, dy=1)
    cols, cn = column_call(col_coords)
    pair = call(pair_kernel, jax.ShapeDtypeStruct((3, 64, ATOMS), jnp.bfloat16), row_coords, other)
    line, sent = line_call([pair, *from_three(pair, "inner")])
    far = []
    for o in OFFSETS[1:]:
        far.append(shift(sent, outer=-o))

    start = start_block.T
    block_mean = jnp.mean(start, axis=1)
    start = start - block_mean[:, None]
    start_hi = lax.reduce_precision(start, 8, 7)
    ones = jnp.ones((128, start.shape[1]), jnp.bfloat16)
    sw = jnp.concatenate([start_hi.astype(jnp.bfloat16), (start - start_hi).astype(jnp.bfloat16), ones], axis=0)
    bm = jnp.concatenate([block_mean, block_mean])[None, :]

    chunks = []
    for rows in ([line], far[:2], far[2:]):
        chunks.append(dist_call(rows, cols, cn, sw))
    n = lax.axis_size("col")
    packed = jax.ShapeDtypeStruct((n, 24, 128), f32)
    sent = call(pack_kernel, packed, *(c[2] for c in chunks), bm)
    got = lax.all_to_all(sent, "col", 0, 0, tiled=True)
    totals = call(owner_kernel, packed, got)
    got = lax.all_to_all(totals, "col", 0, 0, tiled=True)
    left, tc, stat = call(
        panel_kernel,
        (
            jax.ShapeDtypeStruct((144, 32 * n), jnp.bfloat16),
            jax.ShapeDtypeStruct((32 * n, K), f32),
            jax.ShapeDtypeStruct((72, 128), f32),
        ),
        got,
        scratch=[pltpu.VMEM((32 * n, 128), f32)],
    )
    stats = [stat, None, None, None]
    for k in (3, 2, 1):
        stats[k] = swap(stat, k)
    partial = image_call(left, chunks)
    arrived = [partial[0], *exchanged(partial)]
    m, d = call(
        factor_kernel, (jax.ShapeDtypeStruct((64, 128), f32), jax.ShapeDtypeStruct((8, 128), f32)), *stats
    )
    part = call(join_kernel, jax.ShapeDtypeStruct((64, NC), jnp.bfloat16), *arrived, m, d)
    parts = [part, *exchanged([part] * 4)]
    basis = call(basis_kernel, jax.ShapeDtypeStruct((K, 32 * n), f32), tc, m, d)
    image = call(spread_kernel, jax.ShapeDtypeStruct((K, 4 * NC), f32), *parts)
    return (basis.T, image.T)


def solution(mesh):
    in_specs = (P(None, ("row", "col"), None), P(None, "col", None), P("col", None))
    out_specs = (P("row", None), P("col", None))
    return jax.shard_map(body, mesh=mesh, in_specs=in_specs, out_specs=out_specs, check_vma=False)
```

```python
import functools

import jax
import jax.numpy as jnp
from jax import lax
from jax.experimental import pallas as pl
from jax.experimental.pallas import tpu as pltpu
from jax.sharding import PartitionSpec as P


ATOMS = 512
NEWTON = 8
K = 64
TR = 128
TC = 512
SR, SC = 16, 256
EVERY = 6
UNIT_AT = (0, 14, 28, 42, 56, 70)
PANEL_AT = 86
NC = 256
RF = 4096
CF = 32768
HIGHEST = lax.Precision.HIGHEST
OFFSETS = (0, -1, 1, 2)


def centred(coords):
    wide = coords.astype(jnp.float32)
    return wide - jnp.sum(wide, axis=-1, keepdims=True) * (1.0 / ATOMS)


def column_kernel(coords, out, norm):
    total = None
    for k in range(3):
        c = centred(coords[k]).astype(jnp.bfloat16)
        out[k] = c
        w = c.astype(jnp.float32)
        part = jnp.sum(w * w, axis=1, keepdims=True)
        total = part if total is None else total + part
    spread = jnp.broadcast_to(total * (2.0 / ATOMS), (total.shape[0], 128))
    norm[...] = jnp.transpose(spread)[0:8, :]


def column_call(coords):
    frames, step = coords.shape[1], 256
    block = pl.BlockSpec((3, step, ATOMS), lambda i: (0, i, 0))
    return pl.pallas_call(
        column_kernel,
        grid=(frames // step,),
        in_specs=[block],
        out_specs=[block, pl.BlockSpec((8, step), lambda i: (0, i))],
        out_shape=[
            jax.ShapeDtypeStruct(coords.shape, jnp.bfloat16),
            jax.ShapeDtypeStruct((8, frames), jnp.float32),
        ],
        compiler_params=pltpu.CompilerParams(dimension_semantics=("arbitrary",), vmem_limit_bytes=8 << 20),
        cost_estimate=pl.CostEstimate(flops=10 * 3 * frames * ATOMS, bytes_accessed=6 << 20, transcendentals=0),
        name="columns",
    )(pltpu.with_memory_space_constraint(coords, pltpu.HBM))


def own_kernel(mine, out):
    for k in range(3):
        c = centred(mine[k]).astype(jnp.bfloat16).astype(jnp.float32)
        out[k, 0:32, :] = (c * (4.0 / ATOMS)).astype(jnp.bfloat16)


def pair_kernel(other, half, out):
    for k in range(3):
        c = centred(other[k]).astype(jnp.bfloat16).astype(jnp.float32)
        out[k, 0:32, :] = half[k, 0:32, :]
        out[k, 32:64, :] = (c * (4.0 / ATOMS)).astype(jnp.bfloat16)


def line_kernel(p0, p1, p2, p3, out):
    for i, ref in enumerate((p0, p1, p2, p3)):
        out[:, 64 * i : 64 * i + 64, :] = ref[...]


def newton_slice(load, norms, finish):
    g = None
    for k in range(3):
        e0, e1, e2 = load(k, 0), load(k, 1), load(k, 2)
        terms = (e0 * e0, e1 * e1, e2 * e2, e0 * e1, e0 * e2)
        g = terms if g is None else tuple(v + t for v, t in zip(g, terms))
        yield
    g00, g11, g22, g01, g02 = g
    pair = g11 + g22
    q = g00 + pair
    minors = g00 * pair - g01 * g01 - g02 * g02
    c0 = load(1, 1) * load(2, 2) - load(2, 1) * load(1, 2)
    det = load(0, 0) * c0
    minors = minors + c0 * c0
    c1 = load(2, 1) * load(0, 2) - load(0, 1) * load(2, 2)
    det = det + load(1, 0) * c1
    minors = minors + c1 * c1
    c2 = load(0, 1) * load(1, 2) - load(1, 1) * load(0, 2)
    det = det + load(2, 0) * c2
    minors = minors + c2 * c2
    twice = det + det
    x = norms()
    yield
    for _ in range(NEWTON):
        a = x * x - q
        x = (a * (0.75 * a + q) + minors) / (a * x - twice)
        yield
    finish(norms() - x)


def dist_kernel(ns, *refs):
    rows = refs[:ns]
    cols, cn, sw = refs[ns : ns + 3]
    outs, t_out = refs[ns + 3 : ns + 5], refs[ns + 5]
    bufs, rn, kept, sems = refs[ns + 6 : ns + 8], refs[ns + 8], refs[ns + 9], refs[ns + 10]
    nb = rn.shape[0]
    per = nb // ns
    ct = pl.program_id(0)
    last = pl.num_programs(0) - 1

    def frames(rb):
        r = (rb % per) * TR
        return rows[rb // per][:, r : r + TR, :]

    def products(rb, at, buf, units):
        c0 = pl.multiple_of(at * TC, TC)
        lhs = frames(rb).reshape(3 * TR, ATOMS)
        for b, n in units:
            buf[b, :, n * 256 : n * 256 + 256] = lax.dot_general(
                lhs, cols[b, pl.ds(c0 + n * 256, 256), :], (((1,), (1,)), ((), ())), preferred_element_type=jnp.float32
            )

    def newton(rb, buf, r, c):
        def load(a, b):
            return buf[b, a * TR + r : a * TR + r + SR, c : c + SC]

        def norms():
            return rn[rb, r : r + SR, 0:SC] + cn[0:1, c : c + SC]

        def finish(d):
            h = d.astype(jnp.bfloat16)
            kept[ct, rb, 0, r : r + SR, c : c + SC] = h
            kept[ct, rb, 1, r : r + SR, c : c + SC] = (d - h.astype(jnp.float32)).astype(jnp.bfloat16)

        return newton_slice(load, norms, finish)

    def stores(at, rb):
        rows_at = pl.ds(rb * TR, TR)
        return [
            pltpu.make_async_copy(
                kept.at[at, rb, i], outs[i].at[rows_at, pl.ds(pl.multiple_of(at * TC, TC), TC)], sems.at[i, at, rb]
            )
            for i in range(2)
        ]

    def panel(rb):
        w = sw[:, pl.ds(pl.multiple_of(ct * TC, TC), TC)]
        both = kept[ct, rb].reshape(2 * TR, TC)
        t = lax.dot_general(both, w, (((1,), (1,)), ((), ())), preferred_element_type=jnp.float32)
        t_out[rb * TR : rb * TR + TR, :] += t[0:TR] + t[TR : 2 * TR]

    units = [(b, n) for n in range(TC // 256) for b in range(3)]
    slices = [(r, c) for r in range(0, TR, SR) for c in range(0, TC, SC)]

    @pl.when(ct == 0)
    def _():
        t_out[...] = jnp.zeros_like(t_out)
        for rb in range(nb):
            w = frames(rb).astype(jnp.float32)
            n = jnp.sum(jnp.sum(w * w, axis=0), axis=1, keepdims=True) * (2.0 * ATOMS / 16.0)
            rn[rb] = jnp.broadcast_to(n, (TR, SC))
        products(0, 0, bufs[0], units)

    for rb in range(nb):
        after, at = (rb + 1, ct) if rb + 1 < nb else (0, jnp.minimum(ct + 1, last))

        @pl.when(ct <= last)
        def _(rb=rb, after=after, at=at):
            waiting = [newton(rb, bufs[rb % 2], r, c) for r, c in slices]
            running, tick = [], 0
            while waiting or running:
                if waiting and tick % EVERY == 0:
                    running.append(waiting.pop(0))
                if tick in UNIT_AT:
                    j = UNIT_AT.index(tick)
                    products(after, at, bufs[(rb + 1) % 2], units[j : j + 1])
                if tick == PANEL_AT and rb > 0:
                    panel(rb - 1)
                running = [s for s in running if next(s, s) is not s]
                tick += 1

        for copy in stores(ct, rb):
            copy.start()

    panel(nb - 1)

    @pl.when(ct == last)
    def _():
        for at in range(sems.shape[1]):
            for rb in range(nb):
                for copy in stores(at, rb):
                    copy.wait()


def whole(a):
    return pl.BlockSpec(a.shape, lambda *_: (0,) * a.ndim)


def dist_call(sources, cols, cn, sw):
    nc = cols.shape[1]
    r = sum(a.shape[1] for a in sources)
    return pl.pallas_call(
        functools.partial(dist_kernel, len(sources)),
        grid=(nc // TC,),
        in_specs=[whole(a) for a in sources]
        + [whole(cols), pl.BlockSpec((8, TC), lambda c: (0, c)), whole(sw)],
        out_specs=[
            pl.BlockSpec(memory_space=pltpu.HBM),
            pl.BlockSpec(memory_space=pltpu.HBM),
            pl.BlockSpec((r, 256), lambda c: (0, 0)),
        ],
        out_shape=[
            pltpu.HBM((r, nc), jnp.bfloat16),
            pltpu.HBM((r, nc), jnp.bfloat16),
            jax.ShapeDtypeStruct((r, 256), jnp.float32),
        ],
        scratch_shapes=[
            pltpu.VMEM((3, 3 * TR, TC), jnp.float32),
            pltpu.VMEM((3, 3 * TR, TC), jnp.float32),
            pltpu.VMEM((r // TR, TR, SC), jnp.float32),
            pltpu.VMEM((nc // TC, r // TR, 2, TR, TC), jnp.bfloat16),
            pltpu.SemaphoreType.DMA((2, nc // TC, r // TR)),
        ],
        compiler_params=pltpu.CompilerParams(dimension_semantics=("arbitrary",), vmem_limit_bytes=20 << 20),
        cost_estimate=pl.CostEstimate(
            flops=r * nc * 9 * 2 * ATOMS, bytes_accessed=8 << 20, transcendentals=r * nc * NEWTON
        ),
    )(*sources, cols, cn, sw)


PIECES = [(dy, i, o) for dy in range(2) for i in range(4) for o in range(4)]
CHUNK_START = (0, 256, 768)


def place(dy, i, o):
    return (o + 1) // 2, (o == 2) * 256 + (i * 2 + dy) * 32


def owner_of(dy, i, o):
    me, core = lax.axis_index("col"), lax.axis_index("row") % 2
    y, x, z = me // 16, (me // 4) % 4, me % 4
    dx = OFFSETS[o] + core * (OFFSETS[i] - OFFSETS[o])
    dz = OFFSETS[i] + core * (OFFSETS[o] - OFFSETS[i])
    return ((y + dy) % 2) * 16 + ((x + dx + 4) % 4) * 4 + (z + dz + 4) % 4


def lanes(shape):
    return lax.broadcasted_iota(jnp.int32, shape, len(shape) - 1)


def pack_kernel(t0, t1, t2, bm, out):
    ts = (t0, t1, t2)
    lane16, lane8 = lanes((16, 128)), lanes((8, 128))
    means = jnp.broadcast_to(bm[...], (8, 128))
    for piece in PIECES:
        dest = owner_of(*piece)
        chunk, at = place(*piece)
        full, sums = [], []
        for r in (at, at + 16):
            t = ts[chunk][r : r + 16, 0:128]
            full.append(t + pltpu.roll(t, 64, 1))
            sums.append(ts[chunk][r : r + 16, 128:256])
        out[dest, 0:16, :] = jnp.where(lane16 < 64, full[0], full[1])
        ext = jnp.where(lane8 < 16, sums[0][0:8], sums[0][8:16])
        ext = jnp.where(lane8 < 32, ext, sums[1][0:8])
        ext = jnp.where(lane8 < 48, ext, sums[1][8:16])
        out[dest, 16:24, :] = jnp.where(lane8 < 64, ext, means)


def owner_kernel(got, out):
    lane = lanes((8, 128))

    def spread(ext):
        one = lambda k: jnp.broadcast_to(ext[:, k : k + 1], (8, 128))
        return jnp.where(lane < 64, one(0), one(32)), jnp.where(lane < 64, one(16), one(48))

    zero = jnp.zeros((8, 128), jnp.float32)
    a, b, e = zero, zero, zero
    for src in range(got.shape[0]):
        ext = got[src, 16:24, :]
        bm = jnp.where(lane < 64, pltpu.roll(ext, 64, 1), ext)
        r0, r1 = spread(ext)
        a = a + (got[src, 0:8, :] + r0 * bm)
        b = b + (got[src, 8:16, :] + r1 * bm)
        e = e + ext
    bm = jnp.where(lane < 64, pltpu.roll(e, 64, 1), e) * (1.0 / got.shape[0])
    r0, r1 = spread(e)
    a = a - r0 * bm
    b = b - r1 * bm
    sub = lax.broadcasted_iota(jnp.int32, (8, 128), 0)
    y = jnp.sum(r0 * a + r1 * b, axis=0, keepdims=True)
    tot = jnp.sum(r0 + r1, axis=0, keepdims=True)
    ext = jnp.where(sub == 0, jnp.broadcast_to(y, (8, 128)), jnp.broadcast_to(tot, (8, 128)))
    for dst in range(got.shape[0]):
        out[dst, 0:8, :] = a
        out[dst, 8:16, :] = b
        out[dst, 16:24, :] = ext


def panel_kernel(got, left, tc_out, stat, arr):
    n = got.shape[0]
    lane1 = lanes((1, 128))

    def both(v):
        return v + pltpu.roll(v, 64, 1)

    total = jnp.sum(jnp.sum(got[:, 0:16, :], axis=0), axis=0, keepdims=True)
    mean = both(total) * (1.0 / (32 * n))
    ext = jnp.sum(got[:, 16:24, :], axis=0)
    y, rows = both(ext[0:1]), both(ext[1:2])
    x = got[:, 0:16, :] - mean
    flat = x.reshape(n * 16, 128)
    g = lax.dot_general(flat, flat, (((0,), (0,)), ((), ())), precision=HIGHEST, preferred_element_type=jnp.float32)
    stat[0:64, :] = g[0:64, :] + pltpu.roll(g[64:128, :], 64, 1)
    sub = lax.broadcasted_iota(jnp.int32, (8, 128), 0)
    tile = jnp.where(sub == 0, mean, jnp.where(sub == 1, y, rows))
    stat[64:72, :] = jnp.broadcast_to(tile, (8, 128))
    for b in range(n):
        tc_out[b * 32 : b * 32 + 16, :] = x[b, :, 0:64]
        tc_out[b * 32 + 16 : b * 32 + 32, :] = x[b, :, 64:128]
    for piece in PIECES:
        src = owner_of(*piece)
        t = got[src, 0:16, :] - mean
        chunk, r = place(*piece)
        r += CHUNK_START[chunk]
        arr[r : r + 16, :] = t
        arr[r + 16 : r + 32, :] = pltpu.roll(t, 64, 1)
    pt = jnp.transpose(arr[...])[0:64, :]
    h = pt.astype(jnp.bfloat16)
    left[0:64, :] = h
    left[64:128, :] = (pt - h.astype(jnp.float32)).astype(jnp.bfloat16)
    left[128:144, :] = jnp.ones((16, pt.shape[1]), jnp.bfloat16)


def image_kernel(left, h0, l0, h1, l1, h2, l2, o0, o1, o2, o3, late, acc, sems):
    copies = [pltpu.make_async_copy(ref, late.at[i], sems.at[i]) for i, ref in enumerate((h2, l2))]
    for copy in copies:
        copy.start()

    def block(k):
        return pl.ds(pl.multiple_of((lax.axis_index("row") ^ k) * NC, NC), NC)

    for k in range(4):
        total = jnp.zeros((144, NC), jnp.float32)
        for at, refs in zip(CHUNK_START, ((h0, l0), (h1, l1))):
            for ref in refs:
                total += jnp.dot(
                    left[:, at : at + ref.shape[0]], ref[:, block(k)], preferred_element_type=jnp.float32
                )
        acc[k] = total
    for copy in copies:
        copy.wait()
    for k, out in enumerate((o0, o1, o2, o3)):
        total = acc[k]
        for i in range(2):
            total += jnp.dot(left[:, CHUNK_START[2] :], late[i, :, block(k)], preferred_element_type=jnp.float32)
        out[0:64, :] = total[0:64] + total[64:128]
        out[64:72, :] = total[128:136]


def image_call(left, chunks):
    flat = [a for c in chunks for a in c[:2]]
    flat[4:] = [pltpu.with_memory_space_constraint(a, pltpu.HBM) for a in flat[4:]]
    vmem = pl.BlockSpec(memory_space=pltpu.VMEM)
    return pl.pallas_call(
        image_kernel,
        in_specs=[vmem] * 5 + [pl.BlockSpec(memory_space=pltpu.HBM)] * 2,
        out_specs=[vmem] * 4,
        scratch_shapes=[
            pltpu.VMEM((2, *flat[4].shape), jnp.bfloat16),
            pltpu.VMEM((4, 144, NC), jnp.float32),
            pltpu.SemaphoreType.DMA((2,)),
        ],
        out_shape=[jax.ShapeDtypeStruct((72, NC), jnp.float32)] * 4,
        compiler_params=pltpu.CompilerParams(vmem_limit_bytes=12 << 20),
        cost_estimate=pl.CostEstimate(flops=2 * 2 * 256 * 1024 * 1024, bytes_accessed=5 << 20, transcendentals=0),
        name="image",
    )(left, *flat)


def factor_kernel(s0, s1, s2, s3, m_out, d_out):
    stats = (s0, s1, s2, s3)

    def total(lo, hi):
        return (s0[lo:hi, :] + s1[lo:hi, :]) + (s2[lo:hi, :] + s3[lo:hi, :])

    mean = total(64, 65) * 0.25
    offs = [s[64:65, :] - mean for s in stats]
    y = total(65, 66) - mean * total(66, 67)
    sub = lax.broadcasted_iota(jnp.int32, (8, 128), 0)
    deltas = jnp.zeros((8, 128), jnp.float32)
    for k in range(4):
        deltas = jnp.where(sub == k, offs[k], deltas)
    d_out[...] = jnp.where(sub == 4, y * (1.0 / CF), deltas)
    outer = lax.dot_general(
        deltas, deltas, (((0,), (0,)), ((), ())), precision=HIGHEST, preferred_element_type=jnp.float32
    )
    gram = (total(0, 64) + outer[0:64, :] * (RF // 4)) * (1.0 / (16 * RF))
    lane = lanes((64, 128))
    row = lax.broadcasted_iota(jnp.int32, (64, 128), 0)
    a = jnp.where(lane < 64, gram, jnp.where(lane - 64 == row, 1.0, 0.0))
    tiles = [a[8 * t : 8 * t + 8, :] for t in range(8)]
    eighth = lax.broadcasted_iota(jnp.int32, (8, 128), 0)
    for t in range(8):
        cols = [[jnp.broadcast_to(tiles[i][:, 8 * t + j : 8 * t + j + 1], (8, 128)) for i in range(t, 8)] for j in range(8)]
        rest = tiles[t:]
        for j in range(8):
            spread = lambda v: jnp.broadcast_to(v[j : j + 1, :], (8, 128))
            pivot = spread(cols[j][0])
            inv = 1.0 / pivot
            row_j = spread(rest[0])
            m_out[8 * t + j : 8 * t + j + 1, :] = (row_j * (lax.rsqrt(pivot) * -0.25))[0:1, :]
            below = [v * inv for v in cols[j]]
            below[0] = jnp.where(eighth > j, below[0], 0.0)
            for l in range(j + 1, 8):
                top = spread(cols[l][0])
                cols[l] = [v - m * top for v, m in zip(cols[l], below)]
            rest = [v - m * row_j for v, m in zip(rest, below)]
        tiles[t:] = rest


def join_kernel(w, g1, g2, g3, m, d, out):
    parts = (w[0:64] + g1[0:64]) + (g2[0:64] + g3[0:64])
    sub = lax.broadcasted_iota(jnp.int32, (8, NC), 0)
    sums = jnp.where(sub == 4, -1.0, 0.0)
    for k, ref in enumerate((w, g1, g2, g3)):
        sums = jnp.where(sub == k, ref[64:72], sums)
    add = lax.dot_general(
        d[...], sums, (((0,), (0,)), ((), ())), precision=HIGHEST, preferred_element_type=jnp.float32
    )
    inv = pltpu.roll(m[...], 64, 1)[:, 0:64]
    res = jnp.dot(inv, parts + add[0:64], precision=HIGHEST, preferred_element_type=jnp.float32)
    out[...] = (res * (-0.25 / RF**0.5)).astype(jnp.bfloat16)


def basis_kernel(tc, m, d, out):
    inv = pltpu.roll(m[...], 64, 1)[:, 0:64]
    x = tc[...] + d[0:1, 0:64]
    out[...] = lax.dot_general(
        inv, x, (((1,), (1,)), ((), ())), precision=HIGHEST, preferred_element_type=jnp.float32
    )


def spread_kernel(i0, i1, i2, i3, out):
    me = lax.axis_index("row")
    for k, ref in enumerate((i0, i1, i2, i3)):
        at = pl.multiple_of((me ^ k) * NC, NC)
        out[:, pl.ds(at, NC)] = ref[...].astype(jnp.float32)


def call(kernel, outs, *args, scratch=(), **kw):
    return pl.pallas_call(
        kernel,
        out_shape=outs,
        in_specs=[pl.BlockSpec(memory_space=pltpu.VMEM)] * len(args),
        out_specs=jax.tree.map(lambda _: pl.BlockSpec(memory_space=pltpu.VMEM), outs),
        scratch_shapes=scratch,
        compiler_params=pltpu.CompilerParams(vmem_limit_bytes=8 << 20),
        **kw,
    )(*args)


def index(core, lo, y, x, z):
    return (lo * 2 + core) * 32 + ((y % 2) * 4 + x % 4) * 4 + z % 4


DEVICES = [(c, w, y, x, z) for c in range(2) for w in range(2) for y in range(2) for x in range(4) for z in range(4)]


def shift(a, dy=0, inner=0, outer=0):
    pairs = []
    for c, w, y, x, z in DEVICES:
        dx, dz = (inner, outer) if c else (outer, inner)
        pairs.append((index(c, w, y, x, z), index(c, w, y + dy, x + dx, z + dz)))
    return lax.ppermute(a, ("row", "col"), pairs)


def swap(a, k):
    return lax.ppermute(a, "row", [(r, r ^ k) for r in range(4)])


def exchanged(arrays):
    got = {k: swap(arrays[k], k) for k in (3, 2, 1)}
    return [got[k] for k in (1, 2, 3)]


def body(row_coords, col_coords, start_block):
    f32 = jnp.float32
    other = shift(row_coords, dy=1)
    start = start_block.T
    block_mean = jnp.mean(start, axis=1)
    start = start - block_mean[:, None]
    start_hi = lax.reduce_precision(start, 8, 7)
    start_parts = [start_hi.astype(jnp.bfloat16), (start - start_hi).astype(jnp.bfloat16)]
    half = call(own_kernel, jax.ShapeDtypeStruct((3, 32, ATOMS), jnp.bfloat16), row_coords)
    pair = call(pair_kernel, jax.ShapeDtypeStruct((3, 64, ATOMS), jnp.bfloat16), other, half)
    inner, far = [pair], []
    for o in OFFSETS[1:]:
        inner.append(shift(pair, inner=-o))
    cols, cn = column_call(col_coords)
    line = call(line_kernel, jax.ShapeDtypeStruct((3, 256, ATOMS), jnp.bfloat16), *inner)
    for o in OFFSETS[1:]:
        far.append(shift(line, outer=-o))

    ones = jnp.ones((128, start.shape[1]), jnp.bfloat16)
    sw = jnp.concatenate([*start_parts, ones], axis=0)
    bm = jnp.concatenate([block_mean, block_mean])[None, :]

    chunks = []
    for rows in ([line], far[:2], far[2:]):
        chunks.append(dist_call(rows, cols, cn, sw))
    n = lax.axis_size("col")
    packed = jax.ShapeDtypeStruct((n, 24, 128), f32)
    sent = call(pack_kernel, packed, *(c[2] for c in chunks), bm)
    got = lax.all_to_all(sent, "col", 0, 0, tiled=True)
    totals = call(owner_kernel, packed, got)
    got = lax.all_to_all(totals, "col", 0, 0, tiled=True)
    left, tc, stat = call(
        panel_kernel,
        (
            jax.ShapeDtypeStruct((144, 32 * n), jnp.bfloat16),
            jax.ShapeDtypeStruct((32 * n, K), f32),
            jax.ShapeDtypeStruct((72, 128), f32),
        ),
        got,
        scratch=[pltpu.VMEM((32 * n, 128), f32)],
    )
    stats = [stat, None, None, None]
    for k in (3, 2, 1):
        stats[k] = swap(stat, k)
    partial = image_call(left, chunks)
    arrived = [partial[0], *exchanged(partial)]
    m, d = call(
        factor_kernel, (jax.ShapeDtypeStruct((64, 128), f32), jax.ShapeDtypeStruct((8, 128), f32)), *stats
    )
    part = call(join_kernel, jax.ShapeDtypeStruct((64, NC), jnp.bfloat16), *arrived, m, d)
    parts = [part, *exchanged([part] * 4)]
    basis = call(basis_kernel, jax.ShapeDtypeStruct((K, 32 * n), f32), tc, m, d)
    image = call(spread_kernel, jax.ShapeDtypeStruct((K, 4 * NC), f32), *parts)
    return (basis.T, image.T)


def solution(mesh):
    in_specs = (P(None, ("row", "col"), None), P(None, "col", None), P("col", None))
    out_specs = (P("row", None), P("col", None))
    return jax.shard_map(body, mesh=mesh, in_specs=in_specs, out_specs=out_specs, check_vma=False)
```
